32 devices in a mesh: section: 4 (over y, core), dp: 8 (over z, x).
Axes of the slice: x: 2, y: 2, z: 4, core: 2. Of those that a mesh axis runs over, the one named last changes fastest.
Arguments:
- fresh_batches: bfloat16 [3, 512, 4096], P(None, 'dp'), may hold values from -6 to 6
- held_states: bfloat16 [4, 512, 4096], P('section', 'dp'), may hold values from -6 to 6
- section_weight: bfloat16 [4, 4096, 4096], P('section', None, 'dp'), may hold values from -0.09375 to 0.09375
- section_gain: float32 [4, 4096], P('section'), may hold values from 0.25 to 1.75
- final_gain: float32 [4096], replicated, may hold values from 0.3 to 3
- cached_pool: bfloat16 [512, 4096], P('dp'), may hold values from -0.09375 to 0.09375
- route: int32 [8, 64], P('dp'), may hold values from 0 to 63, each once within a row
- queries: bfloat16 [256, 4096], P(('section', 'dp')), may hold values from -0.09375 to 0.09375
- shortlist: int32 [256, 128], P(('section', 'dp')), may hold values from 0 to 63
- teacher: float32 [256, 128], P(('section', 'dp')), may hold values from -16 to 300, as said below
Outputs:
- held_out: bfloat16 [4, 512, 4096], P('section', 'dp')
- losses: float32 [256], P(('section', 'dp'))
- query_grad: float32 [256, 4096], P(('section', 'dp'))
- pool_grad: bfloat16 [512, 4096], P('dp')
The draws below stay inside these ranges and needn't reach their ends.
Inputs may be any that keep to these rules, and one draw needn't show every extreme that they name: `teacher`: reranker scores; on some draws some rows have two entries above the rest.
All inputs are finite; a program needn't handle non-finite values.
Results may differ from the reference program's by a relative error of at most 0.0058.
Values may be sent and summed in bfloat16 or wider, within the bound.
No kernel may reach another device: no remote copies, remote signals or barrier semaphores. Data moves between devices by JAX's collectives and lax.ppermute only.
A program may use at most 64 MiB of HBM per device.

```python
import math
import jax
import jax.numpy as jnp
from jax import lax

D = 4096
SEQ = 128
PASS_MB = 4
TICKS = 3
R = 64
SL = 128
QDEV = 8
TG = 512
Q = 256
POOL = 512
N_SECTION = 4
N_DP = 8


def draw_teacher(key, part):
    key_base = jax.random.fold_in(key, 0)
    rows_total = QDEV * N_SECTION * N_DP
    scores = jnp.clip(jax.random.normal(key_base, (rows_total, SL), jnp.float32) * 2.0, -16.0, 16.0)
    return scores


def touch_ends(result, key, least, top_value):
    longest = result.shape.index(max(result.shape))
    spots = []
    for shift in (0, 1):
        where = [jax.random.randint(jax.random.fold_in(key, axis), (), 0, length) for axis, length in enumerate(result.shape)]
        where[longest] = (where[longest] + shift) % result.shape[longest]
        spots.append(tuple(where))
    return result.at[spots[0]].set(least).at[spots[1]].set(top_value)


def block_scale(key, extent, pieces, least, high):
    gain = 1.0
    for axis_at, parts in pieces:
        draws = jax.random.uniform(jax.random.fold_in(jax.random.fold_in(key, 6), axis_at), (parts,), jnp.float32, least / len(pieces), high / len(pieces))
        gain = gain * jnp.repeat(jnp.exp(draws), extent[axis_at] // parts).reshape((-1,) + (1,) * (len(extent) - 1 - axis_at))
    return gain


def scatter_about(stream_key, dims, deviation, limit, cuts=(), kind=jnp.bfloat16):
    values = deviation * jax.random.normal(stream_key, dims, jnp.float32)
    if cuts:
        values = values * block_scale(stream_key, dims, cuts, -0.22, 0.18)
    return jnp.clip(values, -limit, limit).astype(kind)


def setup_inputs(seed: int = 0) -> dict:
    key_of = jax.random.split(jax.random.key(seed), 11)
    fresh_batches = scatter_about(key_of[0], (TICKS, TG, D), 1.0, 6.0, ((1, 8),))
    held_states = scatter_about(key_of[1], (N_SECTION, TG, D), 1.0, 6.0, ((0, 4), (1, 8)))
    section_weight = scatter_about(key_of[2], (N_SECTION, D, D), D ** -0.5, 0.09375, ((0, 4), (2, 8)))
    section_gain = jnp.clip(1.0 + 0.15 * jax.random.normal(key_of[3], (N_SECTION, D), jnp.float32), 0.25, 1.75)
    final_gain = jnp.clip(jnp.exp(jax.random.uniform(key_of[4], (D,), jnp.float32, math.log(0.3), math.log(3.0))), 0.3, 3.0)
    cached_pool = scatter_about(key_of[5], (POOL, D), D ** -0.5, 0.09375, ((0, 8),))
    route = jax.vmap(lambda own: jax.random.permutation(own, R))(jax.random.split(key_of[6], N_DP)).reshape((N_DP, R)).astype(jnp.int32)
    queries = scatter_about(key_of[7], (Q, D), D ** -0.5, 0.09375, ((0, 32),))
    shortlist = touch_ends(jax.random.randint(key_of[8], (Q, SL), 0, R), jax.random.fold_in(key_of[8], 1), 0, R - 1).astype(jnp.int32)
    teacher = draw_teacher(jax.random.fold_in(key_of[10], 71), 0)
    return dict(fresh_batches=fresh_batches, held_states=held_states, section_weight=section_weight, section_gain=section_gain, final_gain=final_gain, cached_pool=cached_pool, route=route, queries=queries, shortlist=shortlist, teacher=teacher)


epsilon = 1e-06
logit_scale = 20.0

def section_layer(states, weight, section_gain):
    widened = states.astype(jnp.float32)
    inv_rms = lax.rsqrt(lax.optimization_barrier(jnp.mean(widened * widened, axis=-1, keepdims=True)) + epsilon)
    normed = (widened * inv_rms * section_gain).astype(jnp.bfloat16)
    projected = jnp.dot(normed, weight, preferred_element_type=jnp.float32).astype(jnp.bfloat16)
    return (widened + jax.nn.silu(projected.astype(jnp.float32))).astype(jnp.bfloat16)

def embed_rows(last_rows, final_gain):
    scaled = last_rows.astype(jnp.float32) * final_gain
    return (scaled * lax.rsqrt(lax.optimization_barrier(jnp.sum(scaled * scaled, axis=-1, keepdims=True)) + epsilon)).astype(jnp.bfloat16)

def reference(fresh_batches, held_states, section_weight, section_gain, final_gain, cached_pool, route, queries, shortlist, teacher):
    current = held_states
    exit_list = []
    for tick_index in range(TICKS):
        section_outputs = lax.map(lambda packed: section_layer(packed[0], packed[1], packed[2]), (current, section_weight, section_gain))
        last_rows = section_outputs[N_SECTION - 1][SEQ - 1::SEQ]
        exit_list.append(embed_rows(last_rows, final_gain))
        current = jnp.concatenate([fresh_batches[tick_index][None], section_outputs[:-1]], axis=0)
    embedded = jnp.stack(exit_list)
    tok_dev = PASS_MB * SEQ // N_DP
    pool_rows = cached_pool.reshape(N_DP, R, D)
    for passage in range(PASS_MB):
        device = (passage + 1) * SEQ // tok_dev - 1
        pool_rows = pool_rows.at[device, :TICKS].set(embedded[:, passage])
    per_peer = R // N_DP
    outbox = jnp.take_along_axis(pool_rows, route[:, :, None], axis=1)
    received = outbox.reshape(N_DP, N_DP, per_peer, D).transpose(1, 0, 2, 3).reshape(N_DP, R, D)
    query_vecs = queries.reshape(N_SECTION, N_DP, QDEV, D).astype(jnp.float32)
    received_wide = received.astype(jnp.float32)
    all_scores = jnp.einsum('soid,ord->soir', query_vecs, received_wide)
    short_idx = shortlist.reshape(N_SECTION, N_DP, QDEV, SL)
    student = jnp.take_along_axis(all_scores, short_idx, axis=3) * logit_scale
    teacher_logits = teacher.reshape(N_SECTION, N_DP, QDEV, SL)
    student_log = jax.nn.log_softmax(student, axis=-1)
    teacher_log = jax.nn.log_softmax(teacher_logits, axis=-1)
    teacher_prob = jnp.exp(teacher_log)
    losses = lax.optimization_barrier(jnp.sum(teacher_prob * (teacher_log - student_log), axis=-1)).reshape(Q)
    logit_grad = logit_scale * (jnp.exp(student_log) - teacher_prob)
    one_hot = (short_idx[..., None] == jnp.arange(R, dtype=jnp.int32)).astype(jnp.float32)
    pool_logit_grad = jnp.einsum('soij,soijr->soir', logit_grad, one_hot, precision=lax.Precision.HIGHEST)
    query_grad = jnp.einsum('soir,ord->soid', pool_logit_grad, received_wide, precision=lax.Precision.HIGHEST).reshape(Q, D)
    received_grad = jnp.einsum('soir,soid->ord', pool_logit_grad, query_vecs, precision=lax.Precision.HIGHEST).astype(jnp.bfloat16)
    returned = received_grad.reshape(N_DP, N_DP, per_peer, D).transpose(1, 0, 2, 3).reshape(N_DP, R, D)
    row_index = jnp.arange(N_DP, dtype=jnp.int32)[:, None]
    pool_grad = jnp.zeros((N_DP, R, D), jnp.bfloat16).at[row_index, route].set(returned).reshape(N_DP * R, D)
    return (current, losses, query_grad, pool_grad)
```

```python
import jax
import jax.numpy as jnp
from jax import lax
from jax.sharding import PartitionSpec as P

SEQ = 128
TICKS = 3


epsilon = 1e-06
logit_scale = 20.0

AXES = ("section", "dp")


def on_device(
    fresh_batches,
    held_states,
    section_weight,
    section_gain,
    final_gain,
    cached_pool,
    route,
    queries,
    shortlist,
    teacher,
):
    section = lax.axis_index("section")
    sections = lax.axis_size("section")
    dp = lax.axis_index("dp")
    dps = lax.axis_size("dp")
    half = dps // 2
    side, place = dp % 2, dp // 2
    weight = section_weight[0]
    gain = section_gain[0]
    width, cols = weight.shape
    tok = held_states.shape[1]
    pair_rows = 2 * tok

    def send(x, hops):
        return lax.ppermute(
            x, AXES, [(a * dps + i, b * dps + (i ^ flip)) for a, b, flip in hops for i in range(dps)]
        )

    rows = cached_pool.shape[0]
    outbox = jnp.concatenate(
        [
            jnp.take(cached_pool, route[0], axis=0),
            jnp.broadcast_to(route[0].astype(jnp.bfloat16)[:, None], (rows, 128)),
        ],
        axis=1,
    )
    inbox = lax.all_to_all(outbox, "dp", split_axis=0, concat_axis=0, tiled=True)
    owner_queries = lax.all_gather(queries, "section", axis=0, tiled=True)

    gained = (weight.astype(jnp.float32) * gain[:, None]).astype(jnp.bfloat16)
    by_side = gained.reshape(half, 2, cols, cols)
    flips = jnp.where(section == 0, 0, place)
    mine_plain = lax.dynamic_index_in_dim(by_side, side, 1, keepdims=False)
    theirs_plain = lax.dynamic_index_in_dim(by_side, 1 - side, 1, keepdims=False)
    last_full = sections - 1 - TICKS
    theirs_plain = send(theirs_plain, [(a, a, 1) for a in range(sections - 1)])
    order = jnp.arange(half) ^ flips
    inner = half * cols

    def ordered(w):
        return jnp.take(w, order, axis=0).reshape(inner, cols)

    mine_late, theirs_late = ordered(mine_plain), ordered(theirs_plain)
    if last_full == 0:
        mine_first, theirs_first = mine_late, theirs_late
    else:
        mine_first = mine_plain.reshape(inner, cols)
        theirs_first = theirs_plain.reshape(inner, cols)

    def layer(states, mine, theirs, own_at, hops):
        wide = states.astype(jnp.float32)
        square = jnp.sum(wide * wide, axis=-1)
        other_square = send(square, hops)
        other = send(
            jnp.dot(states, theirs, preferred_element_type=jnp.float32).astype(jnp.bfloat16), hops
        )
        own = jnp.dot(states, mine, preferred_element_type=jnp.float32)
        inv_rms = lax.rsqrt((square + other_square) / width + epsilon)
        projected = ((own + other.astype(jnp.float32)) * inv_rms[:, None]).astype(jnp.bfloat16)
        kept = lax.dynamic_slice_in_dim(states, own_at * cols, cols, axis=1).astype(jnp.float32)
        return (kept + jax.nn.silu(projected.astype(jnp.float32))).astype(jnp.bfloat16)

    def token_order(block):
        piled = block.reshape(half, pair_rows, cols)
        return jnp.take(piled, jnp.arange(half) ^ place, axis=0).reshape(block.shape)

    entry = held_states[0]
    for i in range(TICKS - 1):
        entry = jnp.where(section == sections - TICKS + 1 + i, fresh_batches[i], entry)
    used = list(range(last_full + 1)) + list(range(sections - TICKS + 1, sections))
    entry = entry.reshape(tok, half, 2, cols)
    stay = lax.dynamic_index_in_dim(entry, side, 2, keepdims=False).reshape(tok, inner)
    leave = lax.dynamic_index_in_dim(entry, 1 - side, 2, keepdims=False).reshape(tok, inner)
    came = send(leave, [(a, a, 1) for a in used])
    pair = jnp.where(
        side == 0,
        jnp.concatenate([stay, came], axis=0),
        jnp.concatenate([came, stay], axis=0),
    )
    piles = [pair] + [send(pair, [(a, a, 2 * k) for a in used]) for k in range(1, half)]
    states = jnp.concatenate(piles, axis=0)
    fresh_states = [
        send(states, [(sections - TICKS + 1 + i, 0, 0)]) for i in range(TICKS - 1)
    ]
    block = layer(
        states, mine_first, theirs_first, place, [(a, a, 1) for a in range(last_full + 1)]
    )
    block = token_order(block)
    for tick in range(1, TICKS):
        top = last_full + tick
        piles = [send(block, [(a - 1, a, 2 * k) for a in range(1, top + 1)]) for k in range(half)]
        states = jnp.where(section == 0, fresh_states[tick - 1], jnp.concatenate(piles, axis=1))
        block = layer(
            states, mine_late, theirs_late, place - flips, [(a, a, 1) for a in range(top + 1)]
        )
        block = jnp.where(section == 0, token_order(block), block)
    tokens = lax.all_to_all(block, "dp", split_axis=0, concat_axis=1, tiled=True)
    shifted = send(tokens, [(a, a + 1, 0) for a in range(sections - 1)])
    held_out = jnp.where(section == 0, fresh_batches[TICKS - 1], shifted)

    def spread(x):
        return lax.all_to_all(
            jnp.broadcast_to(x[None], (dps, *x.shape)), "dp", split_axis=0, concat_axis=0
        )

    every = SEQ // tok
    ends = spread(held_states[0, tok - 1 :])[every - 1 :: every, 0]
    exits = []
    for tick in range(TICKS):
        wide = ends.astype(jnp.float32)
        inv_rms = lax.rsqrt(jnp.mean(wide * wide, axis=-1, keepdims=True) + epsilon)
        normed = (wide * inv_rms * gain).astype(jnp.bfloat16)
        projected = jnp.dot(normed, weight, preferred_element_type=jnp.float32).astype(jnp.bfloat16)
        kept = lax.dynamic_slice_in_dim(wide, dp * cols, cols, axis=1)
        piece = (kept + jax.nn.silu(projected.astype(jnp.float32))).astype(jnp.bfloat16)
        exits.append(piece)
        if tick < TICKS - 1:
            piece = send(piece, [(a, a + 1, 0) for a in range(sections - 1)])
            ends = jnp.concatenate(list(spread(piece)), axis=1)
    passages = ends.shape[0]
    exit_pieces = lax.all_gather(jnp.concatenate(exits, axis=0), "section", axis=0)[sections - 1]
    exit_rows = jnp.concatenate(list(spread(exit_pieces)), axis=1)
    scaled = exit_rows.astype(jnp.float32) * final_gain
    embedded = (
        scaled * lax.rsqrt(jnp.sum(scaled * scaled, axis=-1, keepdims=True) + epsilon)
    ).astype(jnp.bfloat16)

    per_peer = rows // dps
    source = jnp.arange(rows) // per_peer
    passage = source // every
    is_end = source % every == every - 1
    slot = inbox[:, width].astype(jnp.int32)
    replaced = is_end & (slot < TICKS)
    pick = jnp.where(replaced, slot * passages + passage, -1)
    chosen = (pick[:, None] == jnp.arange(TICKS * passages)).astype(jnp.bfloat16)
    received = jnp.where(
        replaced[:, None],
        jnp.dot(chosen, embedded, preferred_element_type=jnp.float32).astype(jnp.bfloat16),
        inbox[:, :width],
    )
    all_scores = lax.dot_general(
        queries, received, (((1,), (1,)), ((), ())), preferred_element_type=jnp.float32
    )
    listed = shortlist[..., None] == jnp.arange(rows, dtype=jnp.int32)
    student = jnp.sum(jnp.where(listed, all_scores[:, None, :], 0.0), axis=-1) * logit_scale
    student_log = jax.nn.log_softmax(student, axis=-1)
    teacher_log = jax.nn.log_softmax(teacher, axis=-1)
    teacher_prob = jnp.exp(teacher_log)
    losses = jnp.sum(teacher_prob * (teacher_log - student_log), axis=-1)
    logit_grad = logit_scale * (jnp.exp(student_log) - teacher_prob)
    row_grad = jnp.sum(jnp.where(listed, logit_grad[..., None], 0.0), axis=1)
    received_wide = received.astype(jnp.float32)
    owner_grads = lax.all_gather(row_grad, "section", axis=0, tiled=True)
    received_grad = jnp.dot(
        owner_grads.T, owner_queries.astype(jnp.float32), precision=lax.Precision.HIGHEST
    ).astype(jnp.bfloat16)
    query_grad = jnp.dot(row_grad, received_wide, precision=lax.Precision.HIGHEST)
    returned = lax.all_to_all(received_grad, "dp", split_axis=0, concat_axis=0, tiled=True)
    pool_grad = jnp.zeros(returned.shape, jnp.bfloat16).at[route[0]].set(returned)
    return (held_out[None], losses, query_grad, pool_grad)


def solution(mesh):
    return jax.shard_map(
        on_device,
        mesh=mesh,
        in_specs=(
            P(None, "dp", None),
            P("section", "dp", None),
            P("section", None, "dp"),
            P("section", None),
            P(),
            P("dp", None),
            P("dp", None),
            P(("section", "dp"), None),
            P(("section", "dp"), None),
            P(("section", "dp"), None),
        ),
        out_specs=(
            P("section", "dp", None),
            P(("section", "dp")),
            P(("section", "dp"), None),
            P("dp", None),
        ),
        check_vma=False,
    )
```

```python
import jax
import jax.numpy as jnp
from jax import lax
from jax.sharding import PartitionSpec as P


SEQ = 128
TICKS = 3


epsilon = 1e-06
logit_scale = 20.0

AXES = ("section", "dp")


def on_device(
    fresh_batches,
    held_states,
    section_weight,
    section_gain,
    final_gain,
    cached_pool,
    route,
    queries,
    shortlist,
    teacher,
):
    section = lax.axis_index("section")
    sections = lax.axis_size("section")
    dp = lax.axis_index("dp")
    dps = lax.axis_size("dp")
    half = dps // 2
    side, place = dp % 2, dp // 2
    weight = section_weight[0]
    gain = section_gain[0]
    width, cols = weight.shape
    tok = held_states.shape[1]
    pair_rows = 2 * tok

    def send(x, hops):
        return lax.ppermute(
            x, AXES, [(a * dps + i, b * dps + (i ^ flip)) for a, b, flip in hops for i in range(dps)]
        )

    def rows_at(x, index):
        return x.at[index].get(mode="promise_in_bounds")

    by_block = weight.reshape(dps, cols, cols)
    gain_block = gain.reshape(dps, cols, 1)
    flips = jnp.where(section == 0, 0, place)
    inner = half * cols
    last_full = sections - 1 - TICKS

    def gained(order, at):
        index = 2 * order + at
        wide = rows_at(by_block, index).astype(jnp.float32) * rows_at(gain_block, index)
        return wide.astype(jnp.bfloat16).reshape(inner, cols)

    def split_weights(order, firsts):
        mine, theirs = gained(order, side), gained(order, 1 - side)
        rest = [a for a in range(sections - 1) if a not in firsts]
        came = send(theirs, [(a, a, 1) for a in firsts])
        if rest:
            later = send(theirs, [(a, a, 1) for a in rest])
        else:
            later = came
        return mine, came, jnp.where(section <= max(firsts), came, later)

    mine_late, theirs_first, theirs_late = split_weights(
        jnp.arange(half) ^ flips, list(range(last_full + 1))
    )
    mine_first = mine_late
    if last_full > 0:
        mine_first, _, theirs_first = split_weights(
            jnp.arange(half), list(range(last_full + 1))
        )

    entry = held_states[0]
    for i in range(TICKS - 1):
        entry = jnp.where(section == sections - TICKS + 1 + i, fresh_batches[i], entry)
    used = list(range(last_full + 1)) + list(range(sections - TICKS + 1, sections))
    pieces = [entry[:, k * cols : (k + 1) * cols] for k in range(dps)]
    even, odd = jnp.concatenate(pieces[0::2], axis=1), jnp.concatenate(pieces[1::2], axis=1)
    stay, leave = jnp.where(side == 0, even, odd), jnp.where(side == 0, odd, even)
    came = send(leave, [(a, a, 1) for a in used])
    pair = jnp.where(
        side == 0,
        jnp.concatenate([stay, came], axis=0),
        jnp.concatenate([came, stay], axis=0),
    )
    piles = [pair] + [send(pair, [(a, a, 2 * k) for a in used]) for k in range(1, half)]
    states = jnp.concatenate(piles, axis=0)

    rows = cached_pool.shape[0]
    per_peer = rows // dps
    last_token = held_states[0, tok - 1].reshape(1, per_peer, width // per_peer)
    outbox = jnp.concatenate(
        [
            rows_at(cached_pool, route[0]).reshape(dps, per_peer, width),
            jnp.broadcast_to(last_token, (dps, per_peer, width // per_peer)),
            jnp.broadcast_to(
                route[0].astype(jnp.bfloat16).reshape(dps, per_peer, 1), (dps, per_peer, 128)
            ),
        ],
        axis=2,
    )
    inbox = lax.all_to_all(outbox, "dp", split_axis=0, concat_axis=0)
    owner_queries = lax.all_gather(queries, "section", axis=0, tiled=True)

    def layer(states, mine, theirs, own_at, hops):
        wide = states.astype(jnp.float32)
        square = jnp.sum(wide * wide, axis=-1)
        other_square = send(square, hops)
        part = jnp.dot(states, theirs, preferred_element_type=jnp.float32).astype(jnp.bfloat16)
        other = send(part, hops)
        own = jnp.dot(states, mine, preferred_element_type=jnp.float32)
        inv_rms = lax.rsqrt((square + other_square) / width + epsilon)
        projected = ((own + other.astype(jnp.float32)) * inv_rms[:, None]).astype(jnp.bfloat16)
        kept = lax.dynamic_slice_in_dim(states, own_at * cols, cols, axis=1).astype(jnp.float32)
        return (kept + jax.nn.silu(projected.astype(jnp.float32))).astype(jnp.bfloat16)

    def reorder(block, flip):
        piled = block.reshape(half, pair_rows, cols)
        return rows_at(piled, jnp.arange(half) ^ flip).reshape(block.shape)

    fresh_states = []
    for i in range(TICKS - 1):
        fresh_states.append(send(states, [(sections - TICKS + 1 + i, 0, 0)]))
    block = layer(
        states, mine_first, theirs_first, place, [(a, a, 1) for a in range(last_full + 1)]
    )
    block = reorder(block, place)
    for tick in range(1, TICKS):
        top = last_full + tick
        if tick == 1:
            piles = [
                send(block, [(a - 1, a, 2 * k) for a in range(1, top + 1)])
                for k in range(half)
            ]
        else:
            block = send(block, [(a - 1, a, 0) for a in range(1, top + 1)])
            piles = [block] + [
                send(block, [(a, a, 2 * k) for a in range(1, top + 1)])
                for k in range(1, half)
            ]
        states = jnp.where(section == 0, fresh_states[tick - 1], jnp.concatenate(piles, axis=1))
        block = layer(
            states, mine_late, theirs_late, place - flips, [(a, a, 1) for a in range(top + 1)]
        )
        block = reorder(block, place - flips)
    tokens = lax.all_to_all(block, "dp", split_axis=0, concat_axis=1, tiled=True)
    shifted = send(tokens, [(a, a + 1, 0) for a in range(sections - 1)])
    held_out = jnp.where(section == 0, fresh_batches[TICKS - 1], shifted)

    def spread(x):
        pieces = lax.all_to_all(
            jnp.broadcast_to(x[None], (dps, *x.shape)), "dp", split_axis=0, concat_axis=0
        )
        return jnp.transpose(pieces, (1, 0, 2)).reshape(x.shape[0], width)

    every = SEQ // tok
    ends = inbox[every - 1 :: every, :, width : width + width // per_peer].reshape(-1, width)
    exits = []
    for tick in range(TICKS):
        wide = ends.astype(jnp.float32)
        inv_rms = lax.rsqrt(jnp.mean(wide * wide, axis=-1, keepdims=True) + epsilon)
        normed = (wide * inv_rms * gain).astype(jnp.bfloat16)
        projected = jnp.dot(normed, weight, preferred_element_type=jnp.float32)
        projected = projected.astype(jnp.bfloat16).astype(jnp.float32)
        kept = lax.dynamic_slice_in_dim(wide, dp * cols, cols, axis=1)
        piece = (kept + jax.nn.silu(projected)).astype(jnp.bfloat16)
        exits.append(piece)
        if tick < TICKS - 1:
            piece = send(piece, [(a, a + 1, 0) for a in range(sections - 1)])
            ends = spread(piece)
    passages = ends.shape[0]
    exit_pieces = lax.all_gather(jnp.concatenate(exits, axis=0), "section", axis=0)
    exit_rows = spread(exit_pieces[sections - 1])
    scaled = exit_rows.astype(jnp.float32) * final_gain
    embedded = (
        scaled * lax.rsqrt(jnp.sum(scaled * scaled, axis=-1, keepdims=True) + epsilon)
    ).astype(jnp.bfloat16)

    source = jnp.arange(rows) // per_peer
    passage = source // every
    is_end = source % every == every - 1
    slot = inbox[:, :, width + width // per_peer].reshape(rows).astype(jnp.int32)
    replaced = is_end & (slot < TICKS)
    pick = jnp.where(replaced, slot * passages + passage, -1)
    chosen = (pick[:, None] == jnp.arange(TICKS * passages)).astype(jnp.bfloat16)
    received = jnp.where(
        replaced[:, None],
        jnp.dot(chosen, embedded, preferred_element_type=jnp.float32).astype(jnp.bfloat16),
        inbox[:, :, :width].reshape(rows, width),
    )
    all_scores = lax.dot_general(
        queries, received, (((1,), (1,)), ((), ())), preferred_element_type=jnp.float32
    )
    listed = shortlist[..., None] == jnp.arange(rows, dtype=jnp.int32)
    student = jnp.sum(jnp.where(listed, all_scores[:, None, :], 0.0), axis=-1) * logit_scale
    student_log = jax.nn.log_softmax(student, axis=-1)
    teacher_log = jax.nn.log_softmax(teacher, axis=-1)
    teacher_prob = jnp.exp(teacher_log)
    losses = jnp.sum(teacher_prob * (teacher_log - student_log), axis=-1)
    logit_grad = logit_scale * (jnp.exp(student_log) - teacher_prob)
    row_grad = jnp.sum(jnp.where(listed, logit_grad[..., None], 0.0), axis=1)
    received_wide = received.astype(jnp.float32)
    owner_grads = lax.all_gather(row_grad, "section", axis=0, tiled=True)
    received_grad = jnp.dot(
        owner_grads.T, owner_queries.astype(jnp.float32), precision=lax.Precision.HIGHEST
    ).astype(jnp.bfloat16)
    query_grad = jnp.dot(row_grad, received_wide, precision=lax.Precision.HIGHEST)
    returned = lax.all_to_all(received_grad, "dp", split_axis=0, concat_axis=0, tiled=True)
    pool_grad = jnp.zeros(returned.shape, jnp.bfloat16).at[route[0]].set(returned)
    return (held_out[None], losses, query_grad, pool_grad)


def solution(mesh):
    return jax.shard_map(
        on_device,
        mesh=mesh,
        in_specs=(
            P(None, "dp", None),
            P("section", "dp", None),
            P("section", None, "dp"),
            P("section", None),
            P(),
            P("dp", None),
            P("dp", None),
            P(("section", "dp"), None),
            P(("section", "dp"), None),
            P(("section", "dp"), None),
        ),
        out_specs=(
            P("section", "dp", None),
            P(("section", "dp")),
            P(("section", "dp"), None),
            P("dp", None),
        ),
        check_vma=False,
    )
```

```python
import jax
import jax.numpy as jnp
from jax import lax
from jax.sharding import PartitionSpec as P


SEQ = 128
TICKS = 3


epsilon = 1e-06
logit_scale = 20.0

AXES = ("section", "dp")


def on_device(
    fresh_batches,
    held_states,
    section_weight,
    section_gain,
    final_gain,
    cached_pool,
    route,
    queries,
    shortlist,
    teacher,
):
    section = lax.axis_index("section")
    sections = lax.axis_size("section")
    dp = lax.axis_index("dp")
    dps = lax.axis_size("dp")
    half = dps // 2
    side, place = dp % 2, dp // 2
    weight = section_weight[0]
    gain = section_gain[0]
    width, cols = weight.shape
    tok = held_states.shape[1]
    pair_rows = 2 * tok

    def send(x, hops):
        return lax.ppermute(
            x, AXES, [(a * dps + i, b * dps + (i ^ flip)) for a, b, flip in hops for i in range(dps)]
        )

    def rows_at(x, index):
        return x.at[index].get(mode="promise_in_bounds")

    by_block = weight.reshape(dps, cols, cols)
    gain_block = gain.reshape(dps, cols, 1)
    flips = jnp.where(section == 0, 0, place)
    inner = half * cols
    last_full = sections - 1 - TICKS

    def gained(order, at):
        index = 2 * order + at
        wide = rows_at(by_block, index).astype(jnp.float32) * rows_at(gain_block, index)
        return wide.astype(jnp.bfloat16).reshape(inner, cols)

    def split_weights(order, firsts):
        theirs = gained(order, 1 - side)
        mine = gained(order, side)
        rest = [a for a in range(sections - 1) if a not in firsts]
        came = send(theirs, [(a, a, 1) for a in firsts])
        if rest:
            later = send(theirs, [(a, a, 1) for a in rest])
        else:
            later = came
        return mine, came, jnp.where(section <= max(firsts), came, later)

    mine_late, theirs_first, theirs_late = split_weights(
        jnp.arange(half) ^ flips, list(range(last_full + 1))
    )
    mine_first = mine_late
    if last_full > 0:
        mine_first, _, theirs_first = split_weights(
            jnp.arange(half), list(range(last_full + 1))
        )

    entry = held_states[0]
    for i in range(TICKS - 1):
        entry = jnp.where(section == sections - TICKS + 1 + i, fresh_batches[i], entry)
    used = list(range(last_full + 1)) + list(range(sections - TICKS + 1, sections))
    pieces = [entry[:, k * cols : (k + 1) * cols] for k in range(dps)]
    even, odd = jnp.concatenate(pieces[0::2], axis=1), jnp.concatenate(pieces[1::2], axis=1)
    stay, leave = jnp.where(side == 0, even, odd), jnp.where(side == 0, odd, even)
    came = send(leave, [(a, a, 1) for a in used])
    pair = jnp.where(
        side == 0,
        jnp.concatenate([stay, came], axis=0),
        jnp.concatenate([came, stay], axis=0),
    )
    piles = [pair] + [send(pair, [(a, a, 2 * k) for a in used]) for k in range(1, half)]
    states = jnp.concatenate(piles, axis=0)

    rows = cached_pool.shape[0]
    per_peer = rows // dps
    last_token = held_states[0, tok - 1].reshape(1, per_peer, width // per_peer)
    outbox = jnp.concatenate(
        [
            rows_at(cached_pool, route[0]).reshape(dps, per_peer, width),
            jnp.broadcast_to(last_token, (dps, per_peer, width // per_peer)),
            jnp.broadcast_to(
                route[0].astype(jnp.bfloat16).reshape(dps, per_peer, 1), (dps, per_peer, 128)
            ),
        ],
        axis=2,
    )
    inbox = lax.all_to_all(outbox, "dp", split_axis=0, concat_axis=0)
    owner_queries = lax.all_gather(queries, "section", axis=0, tiled=True)

    def layer(states, mine, theirs, own_at, hops):
        wide = states.astype(jnp.float32)
        square = jnp.sum(wide * wide, axis=-1)
        other_square = send(square, hops)
        part = jnp.dot(states, theirs, preferred_element_type=jnp.float32)
        part = part.astype(jnp.bfloat16)
        other = send(part, hops)
        own = jnp.dot(states, mine, preferred_element_type=jnp.float32)
        inv_rms = lax.rsqrt((square + other_square) / width + epsilon)
        projected = ((own + other.astype(jnp.float32)) * inv_rms[:, None]).astype(jnp.bfloat16)
        kept = lax.dynamic_slice_in_dim(states, own_at * cols, cols, axis=1).astype(jnp.float32)
        return (kept + jax.nn.silu(projected.astype(jnp.float32))).astype(jnp.bfloat16)

    def reorder(block, flip):
        piled = block.reshape(half, pair_rows, cols)
        return rows_at(piled, jnp.arange(half) ^ flip).reshape(block.shape)

    fresh_states = []
    for i in range(TICKS - 1):
        fresh_states.append(send(states, [(sections - TICKS + 1 + i, 0, 0)]))
    block = layer(
        states, mine_first, theirs_first, place, [(a, a, 1) for a in range(last_full + 1)]
    )
    block = reorder(block, place)
    for tick in range(1, TICKS):
        top = last_full + tick
        if tick == 1:
            piles = [
                send(block, [(a - 1, a, 2 * k) for a in range(1, top + 1)])
                for k in range(half)
            ]
        else:
            block = send(block, [(a - 1, a, 0) for a in range(1, top + 1)])
            piles = [block] + [
                send(block, [(a, a, 2 * k) for a in range(1, top + 1)])
                for k in range(1, half)
            ]
        states = jnp.where(section == 0, fresh_states[tick - 1], jnp.concatenate(piles, axis=1))
        block = layer(
            states, mine_late, theirs_late, place - flips, [(a, a, 1) for a in range(top + 1)]
        )
        block = reorder(block, place - flips)
    tokens = lax.all_to_all(block, "dp", split_axis=0, concat_axis=1, tiled=True)
    shifted = send(tokens, [(a, a + 1, 0) for a in range(sections - 1)])
    held_out = jnp.where(section == 0, fresh_batches[TICKS - 1], shifted)[None]

    def spread(x):
        pieces = lax.all_to_all(
            jnp.broadcast_to(x[None], (dps, *x.shape)), "dp", split_axis=0, concat_axis=0
        )
        return jnp.transpose(pieces, (1, 0, 2)).reshape(x.shape[0], width)

    every = SEQ // tok
    ends = inbox[every - 1 :: every, :, width : width + width // per_peer].reshape(-1, width)
    exits = []
    for tick in range(TICKS):
        wide = ends.astype(jnp.float32)
        inv_rms = lax.rsqrt(jnp.mean(wide * wide, axis=-1, keepdims=True) + epsilon)
        normed = (wide * inv_rms * gain).astype(jnp.bfloat16)
        projected = jnp.dot(normed, weight, preferred_element_type=jnp.float32)
        projected = projected.astype(jnp.bfloat16).astype(jnp.float32)
        kept = lax.dynamic_slice_in_dim(wide, dp * cols, cols, axis=1)
        piece = (kept + jax.nn.silu(projected)).astype(jnp.bfloat16)
        exits.append(piece)
        if tick < TICKS - 1:
            piece = send(piece, [(a, a + 1, 0) for a in range(sections - 1)])
            ends = spread(piece)
    passages = ends.shape[0]
    exit_pieces = lax.all_gather(jnp.concatenate(exits, axis=0), "section", axis=0)
    exit_rows = spread(exit_pieces[sections - 1])
    scaled = exit_rows.astype(jnp.float32) * final_gain
    embedded = (
        scaled * lax.rsqrt(jnp.sum(scaled * scaled, axis=-1, keepdims=True) + epsilon)
    ).astype(jnp.bfloat16)

    source = jnp.arange(rows) // per_peer
    passage = source // every
    is_end = source % every == every - 1
    slot = inbox[:, :, width + width // per_peer].reshape(rows).astype(jnp.int32)
    replaced = is_end & (slot < TICKS)
    pick = jnp.where(replaced, slot * passages + passage, -1)
    chosen = (pick[:, None] == jnp.arange(TICKS * passages)).astype(jnp.bfloat16)
    received = jnp.where(
        replaced[:, None],
        jnp.dot(chosen, embedded, preferred_element_type=jnp.float32).astype(jnp.bfloat16),
        inbox[:, :, :width].reshape(rows, width),
    )
    all_scores = lax.dot_general(
        queries, received, (((1,), (1,)), ((), ())), preferred_element_type=jnp.float32
    )
    listed = shortlist[..., None] == jnp.arange(rows, dtype=jnp.int32)
    student = jnp.sum(jnp.where(listed, all_scores[:, None, :], 0.0), axis=-1) * logit_scale
    student_log = jax.nn.log_softmax(student, axis=-1)
    teacher_log = jax.nn.log_softmax(teacher, axis=-1)
    teacher_prob = jnp.exp(teacher_log)
    losses = jnp.sum(teacher_prob * (teacher_log - student_log), axis=-1)
    logit_grad = logit_scale * (jnp.exp(student_log) - teacher_prob)
    row_grad = jnp.sum(jnp.where(listed, logit_grad[..., None], 0.0), axis=1)
    received_wide = received.astype(jnp.float32)
    owner_grads = lax.all_gather(row_grad, "section", axis=0, tiled=True)
    received_grad = jnp.dot(
        owner_grads.T, owner_queries.astype(jnp.float32), precision=lax.Precision.HIGHEST
    ).astype(jnp.bfloat16)
    query_grad = jnp.dot(row_grad, received_wide, precision=lax.Precision.HIGHEST)
    returned = lax.all_to_all(received_grad, "dp", split_axis=0, concat_axis=0, tiled=True)
    spots = jnp.arange(rows)
    back = jnp.sum(jnp.where(route[0][None, :] == spots[:, None], spots[None, :], 0), axis=1)
    pool_grad = rows_at(returned, back)
    return (held_out, losses, query_grad, pool_grad)


def solution(mesh):
    return jax.shard_map(
        on_device,
        mesh=mesh,
        in_specs=(
            P(None, "dp", None),
            P("section", "dp", None),
            P("section", None, "dp"),
            P("section", None),
            P(),
            P("dp", None),
            P("dp", None),
            P(("section", "dp"), None),
            P(("section", "dp"), None),
            P(("section", "dp"), None),
        ),
        out_specs=(
            P("section", "dp", None),
            P(("section", "dp")),
            P(("section", "dp"), None),
            P("dp", None),
        ),
        check_vma=False,
    )
```

```python
import functools

import jax
import jax.numpy as jnp
from jax import lax
from jax.experimental import pallas as pl
from jax.experimental.pallas import tpu as pltpu
from jax.sharding import PartitionSpec as P


SEQ = 128
TICKS = 3


epsilon = 1e-06
logit_scale = 20.0

AXES = ("section", "dp")


LANES = 128


def gain_kernel(at_ref, weight_ref, gain_ref, out_ref):
    cols = gain_ref.shape[-1]
    column = jnp.transpose(jnp.broadcast_to(gain_ref[0], (LANES, cols)))[:, :1]
    out_ref[...] = (weight_ref[...].astype(jnp.float32) * column).astype(jnp.bfloat16)


def gained_blocks(weight, gain, at):
    cols = weight.shape[1]
    count = at.shape[0]
    return pl.pallas_call(
        gain_kernel,
        out_shape=jax.ShapeDtypeStruct((count * cols, cols), jnp.bfloat16),
        grid_spec=pltpu.PrefetchScalarGridSpec(
            num_scalar_prefetch=1,
            grid=(count,),
            in_specs=[
                pl.BlockSpec((cols, cols), lambda k, at: (at[k], 0)),
                pl.BlockSpec((1, 1, cols), lambda k, at: (at[k], 0, 0)),
            ],
            out_specs=pl.BlockSpec((cols, cols), lambda k, at: (k, 0)),
        ),
        cost_estimate=pl.CostEstimate(
            flops=count * cols * cols, bytes_accessed=4 * count * cols * cols, transcendentals=0
        ),
    )(at, weight, gain.reshape(-1, 1, cols))


def pick(where_ref, refs, cols):
    *piles, wide = refs
    for k in range(wide.shape[1] // cols):
        block = wide[:, k * cols : (k + 1) * cols]
        yield k, jnp.where(where_ref[0] == 1, block, piles[k][...]) if piles else block


def sent_kernel(where_ref, *refs):
    *states, weight_ref, out_ref, square_ref = refs
    tile, cols = out_ref.shape[0], weight_ref.shape[1]
    total = jnp.zeros((tile, cols), jnp.float32)
    square = jnp.zeros((tile, 1), jnp.float32)
    for k, block in pick(where_ref, states, cols):
        total += jnp.dot(
            block, weight_ref[k * cols : (k + 1) * cols, :], preferred_element_type=jnp.float32
        )
        wide = block.astype(jnp.float32)
        square += jnp.sum(wide * wide, axis=-1, keepdims=True)
    out_ref[:, :cols] = total.astype(jnp.bfloat16)
    high = square.astype(jnp.bfloat16).astype(jnp.float32)
    middle = (square - high).astype(jnp.bfloat16).astype(jnp.float32)
    low = square - high - middle
    lane = lax.broadcasted_iota(jnp.int32, (tile, LANES), 1)
    terms = jnp.where(lane == 0, high, jnp.where(lane == 1, middle, jnp.where(lane == 2, low, 0.0)))
    out_ref[:, cols:] = terms.astype(jnp.bfloat16)
    square_ref[...] = jnp.broadcast_to(square, (tile, LANES))


def kept_kernel(width, where_ref, *refs):
    *states, weight_ref, other_ref, square_ref, wide_ref, out_ref = refs
    _, cols = out_ref.shape
    total = other_ref[:, :cols].astype(jnp.float32)
    for k, block in pick(where_ref, states, cols):
        total += jnp.dot(
            block, weight_ref[k * cols : (k + 1) * cols, :], preferred_element_type=jnp.float32
        )
    square = square_ref[:, :1] + jnp.sum(
        other_ref[:, cols:].astype(jnp.float32), axis=-1, keepdims=True
    )
    projected = (total * lax.rsqrt(square / width + epsilon)).astype(jnp.bfloat16)
    kept = wide_ref[...]
    if len(states) > 1:
        kept = jnp.where(where_ref[0] == 1, kept, states[0][...])
    out_ref[...] = (
        kept.astype(jnp.float32) + jax.nn.silu(projected.astype(jnp.float32))
    ).astype(jnp.bfloat16)


def state_specs(states, tile):
    return [pl.BlockSpec((tile, x.shape[1]), lambda i, at: (i, 0)) for x in states]


def sent_half(at, states, weight, tile):
    tokens = states[0].shape[0]
    inner, cols = weight.shape
    return pl.pallas_call(
        sent_kernel,
        out_shape=(
            jax.ShapeDtypeStruct((tokens, cols + LANES), jnp.bfloat16),
            jax.ShapeDtypeStruct((tokens, LANES), jnp.float32),
        ),
        grid_spec=pltpu.PrefetchScalarGridSpec(
            num_scalar_prefetch=1,
            grid=(tokens // tile,),
            in_specs=state_specs(states, tile)
            + [pl.BlockSpec((inner, cols), lambda i, at: (0, 0))],
            out_specs=(
                pl.BlockSpec((tile, cols + LANES), lambda i, at: (i, 0)),
                pl.BlockSpec((tile, LANES), lambda i, at: (i, 0)),
            ),
        ),
        cost_estimate=pl.CostEstimate(
            flops=2 * tokens * inner * cols,
            bytes_accessed=2 * inner * (tokens + cols),
            transcendentals=0,
        ),
    )(at, *states, weight)


def kept_half(at, states, weight, other, square, width, tile):
    tokens = states[0].shape[0]
    inner, cols = weight.shape
    return pl.pallas_call(
        functools.partial(kept_kernel, width),
        out_shape=jax.ShapeDtypeStruct((tokens, cols), jnp.bfloat16),
        grid_spec=pltpu.PrefetchScalarGridSpec(
            num_scalar_prefetch=1,
            grid=(tokens // tile,),
            in_specs=state_specs(states, tile)
            + [
                pl.BlockSpec((inner, cols), lambda i, at: (0, 0)),
                pl.BlockSpec((tile, cols + LANES), lambda i, at: (i, 0)),
                pl.BlockSpec((tile, LANES), lambda i, at: (i, 0)),
                pl.BlockSpec((tile, cols), lambda i, at: (i, at[1])),
            ],
            out_specs=pl.BlockSpec((tile, cols), lambda i, at: (i ^ at[2], 0)),
        ),
        cost_estimate=pl.CostEstimate(
            flops=2 * tokens * inner * cols,
            bytes_accessed=2 * inner * (tokens + cols),
            transcendentals=tokens * cols,
        ),
    )(at, *states, weight, other, square, states[-1])


def on_device(
    fresh_batches,
    held_states,
    section_weight,
    section_gain,
    final_gain,
    cached_pool,
    route,
    queries,
    shortlist,
    teacher,
):
    section = lax.axis_index("section")
    sections = lax.axis_size("section")
    dp = lax.axis_index("dp")
    dps = lax.axis_size("dp")
    half = dps // 2
    side, place = dp % 2, dp // 2
    weight = section_weight[0]
    gain = section_gain[0]
    width, cols = weight.shape
    tok = held_states.shape[1]
    pair_rows = 2 * tok

    def send(x, hops):
        return lax.ppermute(
            x, AXES, [(a * dps + i, b * dps + (i ^ flip)) for a, b, flip in hops for i in range(dps)]
        )

    def rows_at(x, index):
        return x.at[index].get(mode="promise_in_bounds")

    flips = jnp.where(section == 0, 0, place)
    last_full = sections - 1 - TICKS

    def split_weights(order, firsts):
        theirs = gained_blocks(weight, gain, 2 * order + 1 - side)
        mine = gained_blocks(weight, gain, 2 * order + side)
        rest = [a for a in range(sections - 1) if a not in firsts]
        came = send(theirs, [(a, a, 1) for a in firsts])
        if rest:
            later = send(theirs, [(a, a, 1) for a in rest])
        else:
            later = came
        return mine, came, jnp.where(section <= max(firsts), came, later)

    mine_late, theirs_first, theirs_late = split_weights(
        jnp.arange(half) ^ flips, list(range(last_full + 1))
    )
    mine_first = mine_late
    if last_full > 0:
        mine_first, _, theirs_first = split_weights(
            jnp.arange(half), list(range(last_full + 1))
        )

    entry = held_states[0]
    for i in range(TICKS - 1):
        entry = jnp.where(section == sections - TICKS + 1 + i, fresh_batches[i], entry)
    used = list(range(last_full + 1)) + list(range(sections - TICKS + 1, sections))
    pieces = [entry[:, k * cols : (k + 1) * cols] for k in range(dps)]
    even, odd = jnp.concatenate(pieces[0::2], axis=1), jnp.concatenate(pieces[1::2], axis=1)
    stay, leave = jnp.where(side == 0, even, odd), jnp.where(side == 0, odd, even)
    came = send(leave, [(a, a, 1) for a in used])
    pair = jnp.where(
        side == 0,
        jnp.concatenate([stay, came], axis=0),
        jnp.concatenate([came, stay], axis=0),
    )
    piles = [pair] + [send(pair, [(a, a, 2 * k) for a in used]) for k in range(1, half)]
    states = jnp.concatenate(piles, axis=0)

    rows = cached_pool.shape[0]
    per_peer = rows // dps
    last_token = held_states[0, tok - 1].reshape(1, per_peer, width // per_peer)
    outbox = jnp.concatenate(
        [
            rows_at(cached_pool, route[0]).reshape(dps, per_peer, width),
            jnp.broadcast_to(last_token, (dps, per_peer, width // per_peer)),
            jnp.broadcast_to(
                route[0].astype(jnp.bfloat16).reshape(dps, per_peer, 1), (dps, per_peer, 128)
            ),
        ],
        axis=2,
    )
    inbox = lax.all_to_all(outbox, "dp", split_axis=0, concat_axis=0)
    owner_queries = lax.all_gather(queries, "section", axis=0, tiled=True)

    def layer(states, mine, theirs, at, hops):
        at = jnp.stack([jnp.asarray(x, jnp.int32) for x in at])
        part, square = sent_half(at, states, theirs, pair_rows)
        other = send(part, hops)
        return kept_half(at, states, mine, other, square, width, pair_rows)

    fresh_states = []
    for i in range(TICKS - 1):
        fresh_states.append(send(states, [(sections - TICKS + 1 + i, 0, 0)]))
    block = layer(
        [states],
        mine_first,
        theirs_first,
        (1, place, place),
        [(a, a, 1) for a in range(last_full + 1)],
    )
    first = section == 0
    for tick in range(1, TICKS):
        top = last_full + tick
        if tick == 1:
            piles = [
                send(block, [(a - 1, a, 2 * k) for a in range(1, top + 1)])
                for k in range(half)
            ]
        else:
            block = send(block, [(a - 1, a, 0) for a in range(1, top + 1)])
            piles = [block] + [
                send(block, [(a, a, 2 * k) for a in range(1, top + 1)])
                for k in range(1, half)
            ]
        block = layer(
            piles + [fresh_states[tick - 1]],
            mine_late,
            theirs_late,
            (first, place, jnp.where(first, place, 0)),
            [(a, a, 1) for a in range(top + 1)],
        )
    tokens = lax.all_to_all(block, "dp", split_axis=0, concat_axis=1, tiled=True)
    shifted = send(tokens, [(a, a + 1, 0) for a in range(sections - 1)])
    held_out = jnp.where(section == 0, fresh_batches[TICKS - 1], shifted)[None]

    def spread(x):
        pieces = lax.all_to_all(
            jnp.broadcast_to(x[None], (dps, *x.shape)), "dp", split_axis=0, concat_axis=0
        )
        return jnp.transpose(pieces, (1, 0, 2)).reshape(x.shape[0], width)

    every = SEQ // tok
    ends = inbox[every - 1 :: every, :, width : width + width // per_peer].reshape(-1, width)
    exits = []
    for tick in range(TICKS):
        wide = ends.astype(jnp.float32)
        inv_rms = lax.rsqrt(jnp.mean(wide * wide, axis=-1, keepdims=True) + epsilon)
        normed = (wide * inv_rms * gain).astype(jnp.bfloat16)
        projected = jnp.dot(normed, weight, preferred_element_type=jnp.float32)
        projected = projected.astype(jnp.bfloat16).astype(jnp.float32)
        kept = lax.dynamic_slice_in_dim(wide, dp * cols, cols, axis=1)
        piece = (kept + jax.nn.silu(projected)).astype(jnp.bfloat16)
        exits.append(piece)
        if tick < TICKS - 1:
            piece = send(
                piece, [(a, a + 1, 0) for a in range(sections - TICKS + tick, sections - 1)]
            )
            ends = spread(piece)
    passages = ends.shape[0]
    exit_pieces = lax.all_gather(jnp.concatenate(exits, axis=0), "section", axis=0)
    exit_rows = spread(exit_pieces[sections - 1])
    scaled = exit_rows.astype(jnp.float32) * final_gain
    embedded = (
        scaled * lax.rsqrt(jnp.sum(scaled * scaled, axis=-1, keepdims=True) + epsilon)
    ).astype(jnp.bfloat16)

    source = jnp.arange(rows) // per_peer
    passage = source // every
    is_end = source % every == every - 1
    slot = inbox[:, :, width + width // per_peer].reshape(rows).astype(jnp.int32)
    replaced = is_end & (slot < TICKS)
    pick = jnp.where(replaced, slot * passages + passage, -1)
    chosen = (pick[:, None] == jnp.arange(TICKS * passages)).astype(jnp.bfloat16)
    received = jnp.where(
        replaced[:, None],
        jnp.dot(chosen, embedded, preferred_element_type=jnp.float32).astype(jnp.bfloat16),
        inbox[:, :, :width].reshape(rows, width),
    )
    all_scores = lax.dot_general(
        queries, received, (((1,), (1,)), ((), ())), preferred_element_type=jnp.float32
    )
    listed = shortlist[..., None] == jnp.arange(rows, dtype=jnp.int32)
    student = jnp.sum(jnp.where(listed, all_scores[:, None, :], 0.0), axis=-1) * logit_scale
    student_log = jax.nn.log_softmax(student, axis=-1)
    teacher_log = jax.nn.log_softmax(teacher, axis=-1)
    teacher_prob = jnp.exp(teacher_log)
    losses = jnp.sum(teacher_prob * (teacher_log - student_log), axis=-1)
    logit_grad = logit_scale * (jnp.exp(student_log) - teacher_prob)
    row_grad = jnp.sum(jnp.where(listed, logit_grad[..., None], 0.0), axis=1)
    received_wide = received.astype(jnp.float32)
    owner_grads = lax.all_gather(row_grad, "section", axis=0, tiled=True)
    received_grad = jnp.dot(
        owner_grads.T, owner_queries.astype(jnp.float32), precision=lax.Precision.HIGHEST
    ).astype(jnp.bfloat16)
    query_grad = jnp.dot(row_grad, received_wide, precision=lax.Precision.HIGHEST)
    returned = lax.all_to_all(received_grad, "dp", split_axis=0, concat_axis=0, tiled=True)
    spots = jnp.arange(rows)
    back = jnp.sum(jnp.where(route[0][None, :] == spots[:, None], spots[None, :], 0), axis=1)
    pool_grad = rows_at(returned, back)
    return (held_out, losses, query_grad, pool_grad)


def solution(mesh):
    return jax.shard_map(
        on_device,
        mesh=mesh,
        in_specs=(
            P(None, "dp", None),
            P("section", "dp", None),
            P("section", None, "dp"),
            P("section", None),
            P(),
            P("dp", None),
            P("dp", None),
            P(("section", "dp"), None),
            P(("section", "dp"), None),
            P(("section", "dp"), None),
        ),
        out_specs=(
            P("section", "dp", None),
            P(("section", "dp")),
            P(("section", "dp"), None),
            P("dp", None),
        ),
        check_vma=False,
    )
```

```python
import functools

import jax
import jax.numpy as jnp
from jax import lax
from jax.experimental import pallas as pl
from jax.experimental.pallas import tpu as pltpu
from jax.sharding import PartitionSpec as P


SEQ = 128
TICKS = 3


epsilon = 1e-06
logit_scale = 20.0

AXES = ("section", "dp")


LANES = 128


def gain_kernel(at_ref, weight_ref, gain_ref, out_ref):
    cols = gain_ref.shape[-1]
    column = jnp.transpose(jnp.broadcast_to(gain_ref[0], (LANES, cols)))[:, :1]
    out_ref[...] = (weight_ref[...].astype(jnp.float32) * column).astype(jnp.bfloat16)


def gained_blocks(weight, gain, at):
    cols = weight.shape[1]
    count = at.shape[0]
    return pl.pallas_call(
        gain_kernel,
        out_shape=jax.ShapeDtypeStruct((count * cols, cols), jnp.bfloat16),
        grid_spec=pltpu.PrefetchScalarGridSpec(
            num_scalar_prefetch=1,
            grid=(count,),
            in_specs=[
                pl.BlockSpec((cols, cols), lambda k, at: (at[k], 0)),
                pl.BlockSpec((1, 1, cols), lambda k, at: (at[k], 0, 0)),
            ],
            out_specs=pl.BlockSpec((cols, cols), lambda k, at: (k, 0)),
        ),
        cost_estimate=pl.CostEstimate(
            flops=count * cols * cols, bytes_accessed=4 * count * cols * cols, transcendentals=0
        ),
    )(at, weight, gain.reshape(-1, 1, cols))


def sent_kernel(half, at_ref, *refs):
    *piles, weight_ref, out_ref, square_ref, states_ref = refs
    row_piles, column_piles = piles[:half], piles[half:]
    tile = row_piles[0].shape[0]
    cols = weight_ref.shape[1]

    def by_rows():
        for k, pile in enumerate(row_piles):
            states_ref[k * tile : (k + 1) * tile, :] = pile[...]

    def by_columns():
        for k, pile in enumerate(column_piles):
            states_ref[:, k * cols : (k + 1) * cols] = pile[...]

    if column_piles:
        pl.when(at_ref[0] == 1)(by_rows)
        pl.when(at_ref[0] != 1)(by_columns)
    else:
        by_rows()
    tokens = states_ref.shape[0]
    out_ref[:, :cols] = jnp.dot(
        states_ref[...], weight_ref[...], preferred_element_type=jnp.float32
    ).astype(jnp.bfloat16)
    wide = states_ref[...].astype(jnp.float32)
    square = jnp.sum(wide * wide, axis=-1, keepdims=True)
    high = square.astype(jnp.bfloat16).astype(jnp.float32)
    middle = (square - high).astype(jnp.bfloat16).astype(jnp.float32)
    low = square - high - middle
    lane = lax.broadcasted_iota(jnp.int32, (tokens, LANES), 1)
    terms = jnp.where(lane == 0, high, jnp.where(lane == 1, middle, jnp.where(lane == 2, low, 0.0)))
    out_ref[:, cols:] = terms.astype(jnp.bfloat16)
    square_ref[...] = jnp.broadcast_to(square, (tokens, LANES))


def kept_kernel(width, tile, at_ref, states_ref, weight_ref, other_ref, square_ref, out_ref):
    tokens, cols = out_ref.shape
    own = jnp.dot(states_ref[...], weight_ref[...], preferred_element_type=jnp.float32)
    total = own + other_ref[:, :cols].astype(jnp.float32)
    square = square_ref[:, :1] + jnp.sum(
        other_ref[:, cols:].astype(jnp.float32), axis=-1, keepdims=True
    )
    projected = (total * lax.rsqrt(square / width + epsilon)).astype(jnp.bfloat16)
    kept = states_ref[:, pl.ds(pl.multiple_of(at_ref[1] * cols, LANES), cols)]
    result = (
        kept.astype(jnp.float32) + jax.nn.silu(projected.astype(jnp.float32))
    ).astype(jnp.bfloat16)
    for i in range(tokens // tile):
        spot = pl.multiple_of((i ^ at_ref[2]) * tile, tile)
        out_ref[pl.ds(spot, tile), :] = result[i * tile : (i + 1) * tile]


def specs(count):
    vmem = pl.BlockSpec(memory_space=pltpu.VMEM)
    return [pl.BlockSpec(memory_space=pltpu.SMEM)] + [vmem] * count


def cost(tokens, inner, cols):
    return pl.CostEstimate(
        flops=2 * tokens * inner * cols,
        bytes_accessed=2 * inner * (tokens + cols),
        transcendentals=0,
    )


PARAMS = pltpu.CompilerParams(vmem_limit_bytes=24 << 20)


def sent_half(at, row_piles, column_piles, weight):
    inner, cols = weight.shape
    tokens = len(row_piles) * row_piles[0].shape[0]
    return pl.pallas_call(
        functools.partial(sent_kernel, len(row_piles)),
        out_shape=(
            jax.ShapeDtypeStruct((tokens, cols + LANES), jnp.bfloat16),
            jax.ShapeDtypeStruct((tokens, LANES), jnp.float32),
            jax.ShapeDtypeStruct((tokens, inner), jnp.bfloat16),
        ),
        in_specs=specs(len(row_piles) + len(column_piles) + 1),
        out_specs=(pl.BlockSpec(memory_space=pltpu.VMEM),) * 3,
        compiler_params=PARAMS,
        cost_estimate=cost(tokens, inner, cols),
    )(at, *row_piles, *column_piles, weight)


def kept_half(at, states, weight, other, square, width, tile):
    inner, cols = weight.shape
    tokens = states.shape[0]
    return pl.pallas_call(
        functools.partial(kept_kernel, width, tile),
        out_shape=jax.ShapeDtypeStruct((tokens, cols), jnp.bfloat16),
        in_specs=specs(4),
        out_specs=pl.BlockSpec(memory_space=pltpu.VMEM),
        compiler_params=PARAMS,
        cost_estimate=cost(tokens, inner, cols),
    )(at, states, weight, other, square)


def on_device(
    fresh_batches,
    held_states,
    section_weight,
    section_gain,
    final_gain,
    cached_pool,
    route,
    queries,
    shortlist,
    teacher,
):
    section = lax.axis_index("section")
    sections = lax.axis_size("section")
    dp = lax.axis_index("dp")
    dps = lax.axis_size("dp")
    half = dps // 2
    side, place = dp % 2, dp // 2
    weight = section_weight[0]
    gain = section_gain[0]
    width, cols = weight.shape
    tok = held_states.shape[1]
    pair_rows = 2 * tok

    def send(x, hops):
        return lax.ppermute(
            x, AXES, [(a * dps + i, b * dps + (i ^ flip)) for a, b, flip in hops for i in range(dps)]
        )

    def rows_at(x, index):
        return x.at[index].get(mode="promise_in_bounds")

    flips = jnp.where(section == 0, 0, place)
    last_full = sections - 1 - TICKS

    def split_weights(order, firsts):
        theirs = gained_blocks(weight, gain, 2 * order + 1 - side)
        mine = gained_blocks(weight, gain, 2 * order + side)
        rest = [a for a in range(sections - 1) if a not in firsts]
        came = send(theirs, [(a, a, 1) for a in firsts])
        if rest:
            later = send(theirs, [(a, a, 1) for a in rest])
        else:
            later = came
        return mine, came, jnp.where(section <= max(firsts), came, later)

    mine_late, theirs_first, theirs_late = split_weights(
        jnp.arange(half) ^ flips, list(range(last_full + 1))
    )
    mine_first = mine_late
    if last_full > 0:
        mine_first, _, theirs_first = split_weights(
            jnp.arange(half), list(range(last_full + 1))
        )

    used = list(range(last_full + 1))

    def sides(x):
        pieces = [x[:, k * cols : (k + 1) * cols] for k in range(dps)]
        even, odd = jnp.concatenate(pieces[0::2], axis=1), jnp.concatenate(pieces[1::2], axis=1)
        return jnp.where(side == 0, even, odd), jnp.where(side == 0, odd, even)

    entries = jnp.concatenate([held_states[0], *fresh_batches[: TICKS - 1]], axis=0)
    stay, leave = sides(entries)
    came = send(leave, [(a, a, 1) for a in used])

    def gathered(i, owners):
        here, there = stay[i * tok : (i + 1) * tok], came[i * tok : (i + 1) * tok]
        pair = jnp.where(
            side == 0,
            jnp.concatenate([here, there], axis=0),
            jnp.concatenate([there, here], axis=0),
        )
        return [pair] + [send(pair, [(a, a, 2 * k) for a in owners]) for k in range(1, half)]

    entry_piles = gathered(0, used)
    fresh_piles = []
    for i in range(TICKS - 1):
        fresh_piles.append(gathered(i + 1, [0]))

    rows = cached_pool.shape[0]
    per_peer = rows // dps
    last_token = held_states[0, tok - 1].reshape(1, per_peer, width // per_peer)
    outbox = jnp.concatenate(
        [
            rows_at(cached_pool, route[0]).reshape(dps, per_peer, width),
            jnp.broadcast_to(last_token, (dps, per_peer, width // per_peer)),
            jnp.broadcast_to(
                route[0].astype(jnp.bfloat16).reshape(dps, per_peer, 1), (dps, per_peer, 128)
            ),
        ],
        axis=2,
    )
    inbox = lax.all_to_all(outbox, "dp", split_axis=0, concat_axis=0)
    owner_queries = lax.all_gather(queries, "section", axis=0, tiled=True)

    def layer(row_piles, column_piles, mine, theirs, at, hops):
        at = jnp.stack([jnp.asarray(x, jnp.int32) for x in at])
        part, square, states = sent_half(at, row_piles, column_piles, theirs)
        other = send(part, hops)
        return kept_half(at, states, mine, other, square, width, pair_rows)

    block = layer(
        entry_piles,
        [],
        mine_first,
        theirs_first,
        (1, place, place),
        [(a, a, 1) for a in range(last_full + 1)],
    )
    first = section == 0
    row_order = jnp.where(first, place, 0)
    for tick in range(1, TICKS):
        top = last_full + tick
        if tick == 1:
            piles = [
                send(block, [(a - 1, a, 2 * k) for a in range(1, top + 1)])
                for k in range(half)
            ]
        else:
            block = send(block, [(a - 1, a, 0) for a in range(1, top + 1)])
            piles = [block] + [
                send(block, [(a, a, 2 * k) for a in range(1, top + 1)])
                for k in range(1, half)
            ]
        block = layer(
            fresh_piles[tick - 1],
            piles,
            mine_late,
            theirs_late,
            (first, row_order, row_order),
            [(a, a, 1) for a in range(top + 1)],
        )
    tokens = lax.all_to_all(block, "dp", split_axis=0, concat_axis=1, tiled=True)
    shifted = send(tokens, [(a, a + 1, 0) for a in range(sections - 1)])
    held_out = jnp.where(section == 0, fresh_batches[TICKS - 1], shifted)[None]

    def spread(x):
        pieces = lax.all_to_all(
            jnp.broadcast_to(x[None], (dps, *x.shape)), "dp", split_axis=0, concat_axis=0
        )
        return jnp.transpose(pieces, (1, 0, 2)).reshape(x.shape[0], width)

    every = SEQ // tok
    ends = inbox[every - 1 :: every, :, width : width + width // per_peer].reshape(-1, width)
    exits = []
    for tick in range(TICKS):
        wide = ends.astype(jnp.float32)
        inv_rms = lax.rsqrt(jnp.mean(wide * wide, axis=-1, keepdims=True) + epsilon)
        normed = (wide * inv_rms * gain).astype(jnp.bfloat16)
        projected = jnp.dot(normed, weight, preferred_element_type=jnp.float32)
        projected = projected.astype(jnp.bfloat16).astype(jnp.float32)
        kept = lax.dynamic_slice_in_dim(wide, dp * cols, cols, axis=1)
        piece = (kept + jax.nn.silu(projected)).astype(jnp.bfloat16)
        exits.append(piece)
        if tick < TICKS - 1:
            piece = send(
                piece, [(a, a + 1, 0) for a in range(sections - TICKS + tick, sections - 1)]
            )
            ends = spread(piece)
    passages = ends.shape[0]
    exit_pieces = lax.all_gather(jnp.concatenate(exits, axis=0), "section", axis=0)
    exit_rows = spread(exit_pieces[sections - 1])
    scaled = exit_rows.astype(jnp.float32) * final_gain
    embedded = (
        scaled * lax.rsqrt(jnp.sum(scaled * scaled, axis=-1, keepdims=True) + epsilon)
    ).astype(jnp.bfloat16)

    source = jnp.arange(rows) // per_peer
    passage = source // every
    is_end = source % every == every - 1
    slot = inbox[:, :, width + width // per_peer].reshape(rows).astype(jnp.int32)
    replaced = is_end & (slot < TICKS)
    pick = jnp.where(replaced, slot * passages + passage, -1)
    chosen = (pick[:, None] == jnp.arange(TICKS * passages)).astype(jnp.bfloat16)
    received = jnp.where(
        replaced[:, None],
        jnp.dot(chosen, embedded, preferred_element_type=jnp.float32).astype(jnp.bfloat16),
        inbox[:, :, :width].reshape(rows, width),
    )
    all_scores = lax.dot_general(
        queries, received, (((1,), (1,)), ((), ())), preferred_element_type=jnp.float32
    )
    listed = shortlist[..., None] == jnp.arange(rows, dtype=jnp.int32)
    student = jnp.sum(jnp.where(listed, all_scores[:, None, :], 0.0), axis=-1) * logit_scale
    student_log = jax.nn.log_softmax(student, axis=-1)
    teacher_log = jax.nn.log_softmax(teacher, axis=-1)
    teacher_prob = jnp.exp(teacher_log)
    losses = jnp.sum(teacher_prob * (teacher_log - student_log), axis=-1)
    logit_grad = logit_scale * (jnp.exp(student_log) - teacher_prob)
    row_grad = jnp.sum(jnp.where(listed, logit_grad[..., None], 0.0), axis=1)
    received_wide = received.astype(jnp.float32)
    owner_grads = lax.all_gather(row_grad, "section", axis=0, tiled=True)
    received_grad = jnp.dot(
        owner_grads.T, owner_queries.astype(jnp.float32), precision=lax.Precision.HIGHEST
    ).astype(jnp.bfloat16)
    query_grad = jnp.dot(row_grad, received_wide, precision=lax.Precision.HIGHEST)
    returned = lax.all_to_all(received_grad, "dp", split_axis=0, concat_axis=0, tiled=True)
    spots = jnp.arange(rows)
    back = jnp.sum(jnp.where(route[0][None, :] == spots[:, None], spots[None, :], 0), axis=1)
    pool_grad = rows_at(returned, back)
    return (held_out, losses, query_grad, pool_grad)


def solution(mesh):
    return jax.shard_map(
        on_device,
        mesh=mesh,
        in_specs=(
            P(None, "dp", None),
            P("section", "dp", None),
            P("section", None, "dp"),
            P("section", None),
            P(),
            P("dp", None),
            P("dp", None),
            P(("section", "dp"), None),
            P(("section", "dp"), None),
            P(("section", "dp"), None),
        ),
        out_specs=(
            P("section", "dp", None),
            P(("section", "dp")),
            P(("section", "dp"), None),
            P("dp", None),
        ),
        check_vma=False,
    )
```

```python
import functools

import jax
import jax.numpy as jnp
from jax import lax
from jax.experimental import pallas as pl
from jax.experimental.pallas import tpu as pltpu
from jax.sharding import PartitionSpec as P


SEQ = 128
TICKS = 3


epsilon = 1e-06
logit_scale = 20.0

AXES = ("section", "dp")


LANES = 128


def gain_kernel(at_ref, weight_ref, gain_ref, out_ref):
    cols = gain_ref.shape[-1]
    column = jnp.transpose(jnp.broadcast_to(gain_ref[0], (LANES, cols)))[:, :1]
    out_ref[...] = (weight_ref[...].astype(jnp.float32) * column).astype(jnp.bfloat16)


def gained_blocks(weight, gain, at):
    cols = weight.shape[1]
    count = at.shape[0]
    return pl.pallas_call(
        gain_kernel,
        out_shape=jax.ShapeDtypeStruct((count * cols, cols), jnp.bfloat16),
        grid_spec=pltpu.PrefetchScalarGridSpec(
            num_scalar_prefetch=1,
            grid=(count,),
            in_specs=[
                pl.BlockSpec((cols, cols), lambda k, at: (at[k], 0)),
                pl.BlockSpec((1, 1, cols), lambda k, at: (at[k], 0, 0)),
            ],
            out_specs=pl.BlockSpec((cols, cols), lambda k, at: (k, 0)),
        ),
        cost_estimate=pl.CostEstimate(
            flops=count * cols * cols, bytes_accessed=4 * count * cols * cols, transcendentals=0
        ),
    )(at, weight, gain.reshape(-1, 1, cols))


def sent_kernel(half, at_ref, *refs):
    *piles, weight_ref, out_ref, square_ref, states_ref = refs
    row_piles, column_piles = piles[:half], piles[half:]
    tile = row_piles[0].shape[0]
    cols = weight_ref.shape[1]

    def by_rows():
        for k, pile in enumerate(row_piles):
            states_ref[k * tile : (k + 1) * tile, :] = pile[...]

    def by_columns():
        for k, pile in enumerate(column_piles):
            states_ref[:, k * cols : (k + 1) * cols] = pile[...]

    if column_piles:
        pl.when(at_ref[0] == 1)(by_rows)
        pl.when(at_ref[0] != 1)(by_columns)
    else:
        by_rows()
    tokens = states_ref.shape[0]
    out_ref[:, :cols] = jnp.dot(
        states_ref[...], weight_ref[...], preferred_element_type=jnp.float32
    ).astype(jnp.bfloat16)
    wide = states_ref[...].astype(jnp.float32)
    square = jnp.sum(wide * wide, axis=-1, keepdims=True)
    high = square.astype(jnp.bfloat16).astype(jnp.float32)
    middle = (square - high).astype(jnp.bfloat16).astype(jnp.float32)
    low = square - high - middle
    lane = lax.broadcasted_iota(jnp.int32, (tokens, LANES), 1)
    terms = jnp.where(lane == 0, high, jnp.where(lane == 1, middle, jnp.where(lane == 2, low, 0.0)))
    out_ref[:, cols:] = terms.astype(jnp.bfloat16)
    square_ref[...] = jnp.broadcast_to(square, (tokens, LANES))


def kept_kernel(width, tile, at_ref, states_ref, weight_ref, other_ref, square_ref, out_ref):
    tokens, cols = out_ref.shape
    own = jnp.dot(states_ref[...], weight_ref[...], preferred_element_type=jnp.float32)
    total = own + other_ref[:, :cols].astype(jnp.float32)
    square = square_ref[:, :1] + jnp.sum(
        other_ref[:, cols:].astype(jnp.float32), axis=-1, keepdims=True
    )
    projected = (total * lax.rsqrt(square / width + epsilon)).astype(jnp.bfloat16)
    kept = states_ref[:, pl.ds(pl.multiple_of(at_ref[1] * cols, LANES), cols)]
    result = (
        kept.astype(jnp.float32) + jax.nn.silu(projected.astype(jnp.float32))
    ).astype(jnp.bfloat16)
    for i in range(tokens // tile):
        spot = pl.multiple_of((i ^ at_ref[2]) * tile, tile)
        out_ref[pl.ds(spot, tile), :] = result[i * tile : (i + 1) * tile]


def specs(count):
    vmem = pl.BlockSpec(memory_space=pltpu.VMEM)
    return [pl.BlockSpec(memory_space=pltpu.SMEM)] + [vmem] * count


def cost(tokens, inner, cols):
    return pl.CostEstimate(
        flops=2 * tokens * inner * cols,
        bytes_accessed=2 * inner * (tokens + cols),
        transcendentals=0,
    )


PARAMS = pltpu.CompilerParams(vmem_limit_bytes=24 << 20)


def sent_half(at, row_piles, column_piles, weight):
    inner, cols = weight.shape
    tokens = len(row_piles) * row_piles[0].shape[0]
    return pl.pallas_call(
        functools.partial(sent_kernel, len(row_piles)),
        out_shape=(
            jax.ShapeDtypeStruct((tokens, cols + LANES), jnp.bfloat16),
            jax.ShapeDtypeStruct((tokens, LANES), jnp.float32),
            jax.ShapeDtypeStruct((tokens, inner), jnp.bfloat16),
        ),
        in_specs=specs(len(row_piles) + len(column_piles) + 1),
        out_specs=(pl.BlockSpec(memory_space=pltpu.VMEM),) * 3,
        compiler_params=PARAMS,
        cost_estimate=cost(tokens, inner, cols),
    )(at, *row_piles, *column_piles, weight)


def kept_half(at, states, weight, other, square, width, tile):
    inner, cols = weight.shape
    tokens = states.shape[0]
    return pl.pallas_call(
        functools.partial(kept_kernel, width, tile),
        out_shape=jax.ShapeDtypeStruct((tokens, cols), jnp.bfloat16),
        in_specs=specs(4),
        out_specs=pl.BlockSpec(memory_space=pltpu.VMEM),
        compiler_params=PARAMS,
        cost_estimate=cost(tokens, inner, cols),
    )(at, states, weight, other, square)


def on_device(
    fresh_batches,
    held_states,
    section_weight,
    section_gain,
    final_gain,
    cached_pool,
    route,
    queries,
    shortlist,
    teacher,
):
    section = lax.axis_index("section")
    sections = lax.axis_size("section")
    dp = lax.axis_index("dp")
    dps = lax.axis_size("dp")
    half = dps // 2
    side, place = dp % 2, dp // 2
    weight = section_weight[0]
    gain = section_gain[0]
    width, cols = weight.shape
    tok = held_states.shape[1]
    pair_rows = 2 * tok

    def send(x, hops):
        return lax.ppermute(
            x, AXES, [(a * dps + i, b * dps + (i ^ flip)) for a, b, flip in hops for i in range(dps)]
        )

    def rows_at(x, index):
        return x.at[index].get(mode="promise_in_bounds")

    flips = jnp.where(section == 0, 0, place)
    last_full = sections - 1 - TICKS

    def split_weights(order, firsts):
        theirs = gained_blocks(weight, gain, 2 * order + 1 - side)
        mine = gained_blocks(weight, gain, 2 * order + side)
        rest = [a for a in range(sections - 1) if a not in firsts]
        came = send(theirs, [(a, a, 1) for a in firsts])
        if rest:
            later = send(theirs, [(a, a, 1) for a in rest])
        else:
            later = came
        return mine, came, jnp.where(section <= max(firsts), came, later)

    mine_late, theirs_first, theirs_late = split_weights(
        jnp.arange(half) ^ flips, list(range(last_full + 1))
    )
    mine_first = mine_late
    if last_full > 0:
        mine_first, _, theirs_first = split_weights(
            jnp.arange(half), list(range(last_full + 1))
        )

    helpers = [sections - TICKS + 1 + i for i in range(TICKS - 1)]
    used = list(range(last_full + 1)) + helpers
    entry = held_states[0]
    for helper, fresh in zip(helpers, fresh_batches):
        entry = jnp.where(section == helper, fresh, entry)
    pieces = [entry[:, k * cols : (k + 1) * cols] for k in range(dps)]
    even, odd = jnp.concatenate(pieces[0::2], axis=1), jnp.concatenate(pieces[1::2], axis=1)
    here, leave = jnp.where(side == 0, even, odd), jnp.where(side == 0, odd, even)
    there = send(leave, [(a, a, 1) for a in used])
    pair = jnp.where(
        side == 0,
        jnp.concatenate([here, there], axis=0),
        jnp.concatenate([there, here], axis=0),
    )
    entry_piles = [pair] + [send(pair, [(a, a, 2 * k) for a in used]) for k in range(1, half)]

    rows = cached_pool.shape[0]
    per_peer = rows // dps
    last_token = held_states[0, tok - 1].reshape(1, per_peer, width // per_peer)
    outbox = jnp.concatenate(
        [
            rows_at(cached_pool, route[0]).reshape(dps, per_peer, width),
            jnp.broadcast_to(last_token, (dps, per_peer, width // per_peer)),
            jnp.broadcast_to(
                route[0].astype(jnp.bfloat16).reshape(dps, per_peer, 1), (dps, per_peer, 128)
            ),
        ],
        axis=2,
    )
    inbox = lax.all_to_all(outbox, "dp", split_axis=0, concat_axis=0)
    owner_queries = lax.all_gather(queries, "section", axis=0, tiled=True)

    def layer(row_piles, column_piles, mine, theirs, at, hops):
        at = jnp.stack([jnp.asarray(x, jnp.int32) for x in at])
        part, square, states = sent_half(at, row_piles, column_piles, theirs)
        other = send(part, hops)
        return kept_half(at, states, mine, other, square, width, pair_rows), states

    block, states = layer(
        entry_piles,
        [],
        mine_first,
        theirs_first,
        (1, place, place),
        [(a, a, 1) for a in range(last_full + 1)],
    )
    fresh_states = []
    for helper in helpers:
        fresh_states.append(send(states, [(helper, 0, 0)]))
    first = section == 0
    row_order = jnp.where(first, place, 0)
    for tick in range(1, TICKS):
        top = last_full + tick
        if tick == 1:
            piles = [
                send(block, [(a - 1, a, 2 * k) for a in range(1, top + 1)])
                for k in range(half)
            ]
        else:
            block = send(block, [(a - 1, a, 0) for a in range(1, top + 1)])
            piles = [block] + [
                send(block, [(a, a, 2 * k) for a in range(1, top + 1)])
                for k in range(1, half)
            ]
        block, _ = layer(
            [fresh_states[tick - 1]],
            piles,
            mine_late,
            theirs_late,
            (first, row_order, row_order),
            [(a, a, 1) for a in range(top + 1)],
        )
    tokens = lax.all_to_all(block, "dp", split_axis=0, concat_axis=1, tiled=True)
    shifted = send(tokens, [(a, a + 1, 0) for a in range(sections - 1)])
    held_out = jnp.where(section == 0, fresh_batches[TICKS - 1], shifted)[None]

    def spread(x):
        pieces = lax.all_to_all(
            jnp.broadcast_to(x[None], (dps, *x.shape)), "dp", split_axis=0, concat_axis=0
        )
        return jnp.transpose(pieces, (1, 0, 2)).reshape(x.shape[0], width)

    every = SEQ // tok
    ends = inbox[every - 1 :: every, :, width : width + width // per_peer].reshape(-1, width)
    exits = []
    for tick in range(TICKS):
        wide = ends.astype(jnp.float32)
        inv_rms = lax.rsqrt(jnp.mean(wide * wide, axis=-1, keepdims=True) + epsilon)
        normed = (wide * inv_rms * gain).astype(jnp.bfloat16)
        projected = jnp.dot(normed, weight, preferred_element_type=jnp.float32)
        projected = projected.astype(jnp.bfloat16).astype(jnp.float32)
        kept = lax.dynamic_slice_in_dim(wide, dp * cols, cols, axis=1)
        piece = (kept + jax.nn.silu(projected)).astype(jnp.bfloat16)
        exits.append(piece)
        if tick < TICKS - 1:
            piece = send(
                piece, [(a, a + 1, 0) for a in range(sections - TICKS + tick, sections - 1)]
            )
            ends = spread(piece)
    passages = ends.shape[0]
    exit_pieces = lax.all_gather(jnp.concatenate(exits, axis=0), "section", axis=0)
    exit_rows = spread(exit_pieces[sections - 1])
    scaled = exit_rows.astype(jnp.float32) * final_gain
    embedded = (
        scaled * lax.rsqrt(jnp.sum(scaled * scaled, axis=-1, keepdims=True) + epsilon)
    ).astype(jnp.bfloat16)

    source = jnp.arange(rows) // per_peer
    passage = source // every
    is_end = source % every == every - 1
    slot = inbox[:, :, width + width // per_peer].reshape(rows).astype(jnp.int32)
    replaced = is_end & (slot < TICKS)
    pick = jnp.where(replaced, slot * passages + passage, -1)
    chosen = (pick[:, None] == jnp.arange(TICKS * passages)).astype(jnp.bfloat16)
    received = jnp.where(
        replaced[:, None],
        jnp.dot(chosen, embedded, preferred_element_type=jnp.float32).astype(jnp.bfloat16),
        inbox[:, :, :width].reshape(rows, width),
    )
    all_scores = lax.dot_general(
        queries, received, (((1,), (1,)), ((), ())), preferred_element_type=jnp.float32
    )
    listed = shortlist[..., None] == jnp.arange(rows, dtype=jnp.int32)
    student = jnp.sum(jnp.where(listed, all_scores[:, None, :], 0.0), axis=-1) * logit_scale
    student_log = jax.nn.log_softmax(student, axis=-1)
    teacher_log = jax.nn.log_softmax(teacher, axis=-1)
    teacher_prob = jnp.exp(teacher_log)
    losses = jnp.sum(teacher_prob * (teacher_log - student_log), axis=-1)
    logit_grad = logit_scale * (jnp.exp(student_log) - teacher_prob)
    row_grad = jnp.sum(jnp.where(listed, logit_grad[..., None], 0.0), axis=1)
    received_wide = received.astype(jnp.float32)
    owner_grads = lax.all_gather(row_grad, "section", axis=0, tiled=True)
    received_grad = jnp.dot(
        owner_grads.T, owner_queries.astype(jnp.float32), precision=lax.Precision.HIGHEST
    ).astype(jnp.bfloat16)
    query_grad = jnp.dot(row_grad, received_wide, precision=lax.Precision.HIGHEST)
    returned = lax.all_to_all(received_grad, "dp", split_axis=0, concat_axis=0, tiled=True)
    spots = jnp.arange(rows)
    back = jnp.sum(jnp.where(route[0][None, :] == spots[:, None], spots[None, :], 0), axis=1)
    pool_grad = rows_at(returned, back)
    return (held_out, losses, query_grad, pool_grad)


def solution(mesh):
    return jax.shard_map(
        on_device,
        mesh=mesh,
        in_specs=(
            P(None, "dp", None),
            P("section", "dp", None),
            P("section", None, "dp"),
            P("section", None),
            P(),
            P("dp", None),
            P("dp", None),
            P(("section", "dp"), None),
            P(("section", "dp"), None),
            P(("section", "dp"), None),
        ),
        out_specs=(
            P("section", "dp", None),
            P(("section", "dp")),
            P(("section", "dp"), None),
            P("dp", None),
        ),
        check_vma=False,
    )
```

```python
import functools

import jax
import jax.numpy as jnp
from jax import lax
from jax.experimental import pallas as pl
from jax.experimental.pallas import tpu as pltpu
from jax.sharding import PartitionSpec as P


SEQ = 128
TICKS = 3


epsilon = 1e-06
logit_scale = 20.0

AXES = ("section", "dp")


LANES = 128


def gain_kernel(at_ref, weight_ref, gain_ref, out_ref):
    cols = gain_ref.shape[-1]
    column = jnp.transpose(jnp.broadcast_to(gain_ref[0], (LANES, cols)))[:, :1]
    out_ref[...] = (weight_ref[...].astype(jnp.float32) * column).astype(jnp.bfloat16)


def gained_blocks(weight, gain, at):
    cols = weight.shape[1]
    count = at.shape[0]
    return pl.pallas_call(
        gain_kernel,
        out_shape=jax.ShapeDtypeStruct((count * cols, cols), jnp.bfloat16),
        grid_spec=pltpu.PrefetchScalarGridSpec(
            num_scalar_prefetch=1,
            grid=(count,),
            in_specs=[
                pl.BlockSpec((cols, cols), lambda k, at: (at[k], 0)),
                pl.BlockSpec((1, 1, cols), lambda k, at: (at[k], 0, 0)),
            ],
            out_specs=pl.BlockSpec((cols, cols), lambda k, at: (k, 0)),
        ),
        cost_estimate=pl.CostEstimate(
            flops=count * cols * cols, bytes_accessed=4 * count * cols * cols, transcendentals=0
        ),
    )(at, weight, gain.reshape(-1, 1, cols))


def sent_kernel(half, at_ref, *refs):
    *piles, weight_ref, out_ref, square_ref, states_ref = refs
    row_piles, column_piles = piles[:half], piles[half:]
    tile = row_piles[0].shape[0]
    cols = weight_ref.shape[1]

    def by_rows():
        for k, pile in enumerate(row_piles):
            states_ref[k * tile : (k + 1) * tile, :] = pile[...]

    def by_columns():
        for k, pile in enumerate(column_piles):
            states_ref[:, k * cols : (k + 1) * cols] = pile[...]

    if column_piles:
        pl.when(at_ref[0] == 1)(by_rows)
        pl.when(at_ref[0] != 1)(by_columns)
    else:
        by_rows()
    tokens = states_ref.shape[0]
    out_ref[:, :cols] = jnp.dot(
        states_ref[...], weight_ref[...], preferred_element_type=jnp.float32
    ).astype(jnp.bfloat16)
    wide = states_ref[...].astype(jnp.float32)
    square = jnp.sum(wide * wide, axis=-1, keepdims=True)
    high = square.astype(jnp.bfloat16).astype(jnp.float32)
    middle = (square - high).astype(jnp.bfloat16).astype(jnp.float32)
    low = square - high - middle
    lane = lax.broadcasted_iota(jnp.int32, (tokens, LANES), 1)
    terms = jnp.where(lane == 0, high, jnp.where(lane == 1, middle, jnp.where(lane == 2, low, 0.0)))
    out_ref[:, cols:] = terms.astype(jnp.bfloat16)
    square_ref[...] = jnp.broadcast_to(square, (tokens, LANES))


def kept_kernel(width, tile, at_ref, states_ref, weight_ref, other_ref, square_ref, out_ref):
    tokens, cols = out_ref.shape
    own = jnp.dot(states_ref[...], weight_ref[...], preferred_element_type=jnp.float32)
    total = own + other_ref[:, :cols].astype(jnp.float32)
    square = square_ref[:, :1] + jnp.sum(
        other_ref[:, cols:].astype(jnp.float32), axis=-1, keepdims=True
    )
    projected = (total * lax.rsqrt(square / width + epsilon)).astype(jnp.bfloat16)
    kept = states_ref[:, pl.ds(pl.multiple_of(at_ref[1] * cols, LANES), cols)]
    result = (
        kept.astype(jnp.float32) + jax.nn.silu(projected.astype(jnp.float32))
    ).astype(jnp.bfloat16)
    for i in range(tokens // tile):
        spot = pl.multiple_of((i ^ at_ref[2]) * tile, tile)
        out_ref[pl.ds(spot, tile), :] = result[i * tile : (i + 1) * tile]


def specs(count):
    vmem = pl.BlockSpec(memory_space=pltpu.VMEM)
    return [pl.BlockSpec(memory_space=pltpu.SMEM)] + [vmem] * count


def cost(tokens, inner, cols):
    return pl.CostEstimate(
        flops=2 * tokens * inner * cols,
        bytes_accessed=2 * inner * (tokens + cols),
        transcendentals=0,
    )


PARAMS = pltpu.CompilerParams(vmem_limit_bytes=24 << 20)


def sent_half(at, row_piles, column_piles, weight):
    inner, cols = weight.shape
    tokens = len(row_piles) * row_piles[0].shape[0]
    return pl.pallas_call(
        functools.partial(sent_kernel, len(row_piles)),
        out_shape=(
            jax.ShapeDtypeStruct((tokens, cols + LANES), jnp.bfloat16),
            jax.ShapeDtypeStruct((tokens, LANES), jnp.float32),
            jax.ShapeDtypeStruct((tokens, inner), jnp.bfloat16),
        ),
        in_specs=specs(len(row_piles) + len(column_piles) + 1),
        out_specs=(pl.BlockSpec(memory_space=pltpu.VMEM),) * 3,
        compiler_params=PARAMS,
        cost_estimate=cost(tokens, inner, cols),
    )(at, *row_piles, *column_piles, weight)


def kept_half(at, states, weight, other, square, width, tile):
    inner, cols = weight.shape
    tokens = states.shape[0]
    return pl.pallas_call(
        functools.partial(kept_kernel, width, tile),
        out_shape=jax.ShapeDtypeStruct((tokens, cols), jnp.bfloat16),
        in_specs=specs(4),
        out_specs=pl.BlockSpec(memory_space=pltpu.VMEM),
        compiler_params=PARAMS,
        cost_estimate=cost(tokens, inner, cols),
    )(at, states, weight, other, square)


def on_device(
    fresh_batches,
    held_states,
    section_weight,
    section_gain,
    final_gain,
    cached_pool,
    route,
    queries,
    shortlist,
    teacher,
):
    section = lax.axis_index("section")
    sections = lax.axis_size("section")
    dp = lax.axis_index("dp")
    dps = lax.axis_size("dp")
    half = dps // 2
    side, place = dp % 2, dp // 2
    weight = section_weight[0]
    gain = section_gain[0]
    width, cols = weight.shape
    tok = held_states.shape[1]
    pair_rows = 2 * tok

    def send(x, hops):
        return lax.ppermute(
            x, AXES, [(a * dps + i, b * dps + (i ^ flip)) for a, b, flip in hops for i in range(dps)]
        )

    def rows_at(x, index):
        return x.at[index].get(mode="promise_in_bounds")

    flips = jnp.where(section == 0, 0, place)
    last_full = sections - 1 - TICKS

    def split_weights(order, firsts):
        theirs = gained_blocks(weight, gain, 2 * order + 1 - side)
        mine = gained_blocks(weight, gain, 2 * order + side)
        rest = [a for a in range(sections - 1) if a not in firsts]
        came = send(theirs, [(a, a, 1) for a in firsts])
        if rest:
            later = send(theirs, [(a, a, 1) for a in rest])
        else:
            later = came
        return mine, came, jnp.where(section <= max(firsts), came, later)

    mine_late, theirs_first, theirs_late = split_weights(
        jnp.arange(half) ^ flips, list(range(last_full + 1))
    )
    mine_first = mine_late
    if last_full > 0:
        mine_first, _, theirs_first = split_weights(
            jnp.arange(half), list(range(last_full + 1))
        )

    helper = sections - TICKS + 1
    used = list(range(last_full + 1)) + [helper]

    def sides(x):
        pieces = [x[:, k * cols : (k + 1) * cols] for k in range(dps)]
        even, odd = jnp.concatenate(pieces[0::2], axis=1), jnp.concatenate(pieces[1::2], axis=1)
        return jnp.where(side == 0, even, odd), jnp.where(side == 0, odd, even)

    def gathered(x, owners):
        here, leave = sides(x)
        there = send(leave, [(a, a, 1) for a in owners])
        pair = jnp.where(
            side == 0,
            jnp.concatenate([here, there], axis=0),
            jnp.concatenate([there, here], axis=0),
        )
        return [pair] + [send(pair, [(a, a, 2 * k) for a in owners]) for k in range(1, half)]

    entry = jnp.where(section == helper, fresh_batches[0], held_states[0])
    entry_piles = gathered(entry, used)
    fresh_piles = [gathered(fresh_batches[i], [0]) for i in range(1, TICKS - 1)]

    rows = cached_pool.shape[0]
    per_peer = rows // dps
    last_token = held_states[0, tok - 1].reshape(1, per_peer, width // per_peer)
    outbox = jnp.concatenate(
        [
            rows_at(cached_pool, route[0]).reshape(dps, per_peer, width),
            jnp.broadcast_to(last_token, (dps, per_peer, width // per_peer)),
            jnp.broadcast_to(
                route[0].astype(jnp.bfloat16).reshape(dps, per_peer, 1), (dps, per_peer, 128)
            ),
        ],
        axis=2,
    )
    inbox = lax.all_to_all(outbox, "dp", split_axis=0, concat_axis=0)
    owner_queries = lax.all_gather(queries, "section", axis=0, tiled=True)

    def layer(row_piles, column_piles, mine, theirs, at, hops):
        at = jnp.stack([jnp.asarray(x, jnp.int32) for x in at])
        part, square, states = sent_half(at, row_piles, column_piles, theirs)
        other = send(part, hops)
        return kept_half(at, states, mine, other, square, width, pair_rows), states

    block, states = layer(
        entry_piles,
        [],
        mine_first,
        theirs_first,
        (1, place, place),
        [(a, a, 1) for a in range(last_full + 1)],
    )
    fresh_piles.insert(0, [send(states, [(helper, 0, 0)])])
    first = section == 0
    row_order = jnp.where(first, place, 0)
    for tick in range(1, TICKS):
        top = last_full + tick
        if tick == 1:
            piles = [
                send(block, [(a - 1, a, 2 * k) for a in range(1, top + 1)])
                for k in range(half)
            ]
        else:
            block = send(block, [(a - 1, a, 0) for a in range(1, top + 1)])
            piles = [block] + [
                send(block, [(a, a, 2 * k) for a in range(1, top + 1)])
                for k in range(1, half)
            ]
        block, _ = layer(
            fresh_piles[tick - 1],
            piles,
            mine_late,
            theirs_late,
            (first, row_order, row_order),
            [(a, a, 1) for a in range(top + 1)],
        )
    tokens = lax.all_to_all(block, "dp", split_axis=0, concat_axis=1, tiled=True)
    shifted = send(tokens, [(a, a + 1, 0) for a in range(sections - 1)])
    held_out = jnp.where(section == 0, fresh_batches[TICKS - 1], shifted)[None]

    def spread(x):
        pieces = lax.all_to_all(
            jnp.broadcast_to(x[None], (dps, *x.shape)), "dp", split_axis=0, concat_axis=0
        )
        return jnp.transpose(pieces, (1, 0, 2)).reshape(x.shape[0], width)

    every = SEQ // tok
    ends = inbox[every - 1 :: every, :, width : width + width // per_peer].reshape(-1, width)
    exits = []
    for tick in range(TICKS):
        wide = ends.astype(jnp.float32)
        inv_rms = lax.rsqrt(jnp.mean(wide * wide, axis=-1, keepdims=True) + epsilon)
        normed = (wide * inv_rms * gain).astype(jnp.bfloat16)
        projected = jnp.dot(normed, weight, preferred_element_type=jnp.float32)
        projected = projected.astype(jnp.bfloat16).astype(jnp.float32)
        kept = lax.dynamic_slice_in_dim(wide, dp * cols, cols, axis=1)
        piece = (kept + jax.nn.silu(projected)).astype(jnp.bfloat16)
        exits.append(piece)
        if tick < TICKS - 1:
            piece = send(
                piece, [(a, a + 1, 0) for a in range(sections - TICKS + tick, sections - 1)]
            )
            ends = spread(piece)
    passages = ends.shape[0]
    exit_pieces = lax.all_gather(jnp.concatenate(exits, axis=0), "section", axis=0)
    exit_rows = spread(exit_pieces[sections - 1])
    scaled = exit_rows.astype(jnp.float32) * final_gain
    embedded = (
        scaled * lax.rsqrt(jnp.sum(scaled * scaled, axis=-1, keepdims=True) + epsilon)
    ).astype(jnp.bfloat16)

    source = jnp.arange(rows) // per_peer
    passage = source // every
    is_end = source % every == every - 1
    slot = inbox[:, :, width + width // per_peer].reshape(rows).astype(jnp.int32)
    replaced = is_end & (slot < TICKS)
    pick = jnp.where(replaced, slot * passages + passage, -1)
    chosen = (pick[:, None] == jnp.arange(TICKS * passages)).astype(jnp.bfloat16)
    received = jnp.where(
        replaced[:, None],
        jnp.dot(chosen, embedded, preferred_element_type=jnp.float32).astype(jnp.bfloat16),
        inbox[:, :, :width].reshape(rows, width),
    )
    all_scores = lax.dot_general(
        queries, received, (((1,), (1,)), ((), ())), preferred_element_type=jnp.float32
    )
    listed = shortlist[..., None] == jnp.arange(rows, dtype=jnp.int32)
    student = jnp.sum(jnp.where(listed, all_scores[:, None, :], 0.0), axis=-1) * logit_scale
    student_log = jax.nn.log_softmax(student, axis=-1)
    teacher_log = jax.nn.log_softmax(teacher, axis=-1)
    teacher_prob = jnp.exp(teacher_log)
    losses = jnp.sum(teacher_prob * (teacher_log - student_log), axis=-1)
    logit_grad = logit_scale * (jnp.exp(student_log) - teacher_prob)
    row_grad = jnp.sum(jnp.where(listed, logit_grad[..., None], 0.0), axis=1)
    received_wide = received.astype(jnp.float32)
    owner_grads = lax.all_gather(row_grad, "section", axis=0, tiled=True)
    received_grad = jnp.dot(
        owner_grads.T, owner_queries.astype(jnp.float32), precision=lax.Precision.HIGHEST
    ).astype(jnp.bfloat16)
    query_grad = jnp.dot(row_grad, received_wide, precision=lax.Precision.HIGHEST)
    returned = lax.all_to_all(received_grad, "dp", split_axis=0, concat_axis=0, tiled=True)
    spots = jnp.arange(rows)
    back = jnp.sum(jnp.where(route[0][None, :] == spots[:, None], spots[None, :], 0), axis=1)
    pool_grad = rows_at(returned, back)
    return (held_out, losses, query_grad, pool_grad)


def solution(mesh):
    return jax.shard_map(
        on_device,
        mesh=mesh,
        in_specs=(
            P(None, "dp", None),
            P("section", "dp", None),
            P("section", None, "dp"),
            P("section", None),
            P(),
            P("dp", None),
            P("dp", None),
            P(("section", "dp"), None),
            P(("section", "dp"), None),
            P(("section", "dp"), None),
        ),
        out_specs=(
            P("section", "dp", None),
            P(("section", "dp")),
            P(("section", "dp"), None),
            P("dp", None),
        ),
        check_vma=False,
    )
```

```python
import functools

import jax
import jax.numpy as jnp
from jax import lax
from jax.experimental import pallas as pl
from jax.experimental.pallas import tpu as pltpu
from jax.sharding import PartitionSpec as P


SEQ = 128
TICKS = 3


epsilon = 1e-06
logit_scale = 20.0

AXES = ("section", "dp")


LANES = 128


def gain_kernel(at_ref, weight_ref, gain_ref, out_ref):
    cols = gain_ref.shape[-1]
    column = jnp.transpose(jnp.broadcast_to(gain_ref[0], (LANES, cols)))[:, :1]
    out_ref[...] = (weight_ref[...].astype(jnp.float32) * column).astype(jnp.bfloat16)


def gained_blocks(weight, gain, at):
    cols = weight.shape[1]
    count = at.shape[0]
    return pl.pallas_call(
        gain_kernel,
        out_shape=jax.ShapeDtypeStruct((count * cols, cols), jnp.bfloat16),
        grid_spec=pltpu.PrefetchScalarGridSpec(
            num_scalar_prefetch=1,
            grid=(count,),
            in_specs=[
                pl.BlockSpec((cols, cols), lambda k, at: (at[k], 0)),
                pl.BlockSpec((1, 1, cols), lambda k, at: (at[k], 0, 0)),
            ],
            out_specs=pl.BlockSpec((cols, cols), lambda k, at: (k, 0)),
        ),
        cost_estimate=pl.CostEstimate(
            flops=count * cols * cols, bytes_accessed=4 * count * cols * cols, transcendentals=0
        ),
    )(at, weight, gain.reshape(-1, 1, cols))


def sent_kernel(half, at_ref, *refs):
    *piles, weight_ref, out_ref, square_ref, states_ref = refs
    row_piles, column_piles = piles[:half], piles[half:]
    tile = row_piles[0].shape[0]
    cols = weight_ref.shape[1]

    def by_rows():
        for k, pile in enumerate(row_piles):
            states_ref[k * tile : (k + 1) * tile, :] = pile[...]

    def by_columns():
        for k, pile in enumerate(column_piles):
            states_ref[:, k * cols : (k + 1) * cols] = pile[...]

    if column_piles:
        pl.when(at_ref[0] == 1)(by_rows)
        pl.when(at_ref[0] != 1)(by_columns)
    else:
        by_rows()
    tokens = states_ref.shape[0]
    out_ref[:, :cols] = jnp.dot(
        states_ref[...], weight_ref[...], preferred_element_type=jnp.float32
    ).astype(jnp.bfloat16)
    wide = states_ref[...].astype(jnp.float32)
    square = jnp.sum(wide * wide, axis=-1, keepdims=True)
    high = square.astype(jnp.bfloat16).astype(jnp.float32)
    middle = (square - high).astype(jnp.bfloat16).astype(jnp.float32)
    low = square - high - middle
    lane = lax.broadcasted_iota(jnp.int32, (tokens, LANES), 1)
    terms = jnp.where(lane == 0, high, jnp.where(lane == 1, middle, jnp.where(lane == 2, low, 0.0)))
    out_ref[:, cols:] = terms.astype(jnp.bfloat16)
    square_ref[...] = jnp.broadcast_to(square, (tokens, LANES))


def kept_kernel(width, tile, at_ref, states_ref, weight_ref, other_ref, square_ref, out_ref):
    tokens, cols = out_ref.shape
    own = jnp.dot(states_ref[...], weight_ref[...], preferred_element_type=jnp.float32)
    total = own + other_ref[:, :cols].astype(jnp.float32)
    square = square_ref[:, :1] + jnp.sum(
        other_ref[:, cols:].astype(jnp.float32), axis=-1, keepdims=True
    )
    projected = (total * lax.rsqrt(square / width + epsilon)).astype(jnp.bfloat16)
    kept = states_ref[:, pl.ds(pl.multiple_of(at_ref[1] * cols, LANES), cols)]
    result = (
        kept.astype(jnp.float32) + jax.nn.silu(projected.astype(jnp.float32))
    ).astype(jnp.bfloat16)
    for i in range(tokens // tile):
        spot = pl.multiple_of((i ^ at_ref[2]) * tile, tile)
        out_ref[pl.ds(spot, tile), :] = result[i * tile : (i + 1) * tile]


def specs(count):
    vmem = pl.BlockSpec(memory_space=pltpu.VMEM)
    return [pl.BlockSpec(memory_space=pltpu.SMEM)] + [vmem] * count


def cost(tokens, inner, cols):
    return pl.CostEstimate(
        flops=2 * tokens * inner * cols,
        bytes_accessed=2 * inner * (tokens + cols),
        transcendentals=0,
    )


PARAMS = pltpu.CompilerParams(vmem_limit_bytes=24 << 20)


def sent_half(at, row_piles, column_piles, weight):
    inner, cols = weight.shape
    tokens = len(row_piles) * row_piles[0].shape[0]
    return pl.pallas_call(
        functools.partial(sent_kernel, len(row_piles)),
        out_shape=(
            jax.ShapeDtypeStruct((tokens, cols + LANES), jnp.bfloat16),
            jax.ShapeDtypeStruct((tokens, LANES), jnp.float32),
            jax.ShapeDtypeStruct((tokens, inner), jnp.bfloat16),
        ),
        in_specs=specs(len(row_piles) + len(column_piles) + 1),
        out_specs=(pl.BlockSpec(memory_space=pltpu.VMEM),) * 3,
        compiler_params=PARAMS,
        cost_estimate=cost(tokens, inner, cols),
    )(at, *row_piles, *column_piles, weight)


def kept_half(at, states, weight, other, square, width, tile):
    inner, cols = weight.shape
    tokens = states.shape[0]
    return pl.pallas_call(
        functools.partial(kept_kernel, width, tile),
        out_shape=jax.ShapeDtypeStruct((tokens, cols), jnp.bfloat16),
        in_specs=specs(4),
        out_specs=pl.BlockSpec(memory_space=pltpu.VMEM),
        compiler_params=PARAMS,
        cost_estimate=cost(tokens, inner, cols),
    )(at, states, weight, other, square)


def on_device(
    fresh_batches,
    held_states,
    section_weight,
    section_gain,
    final_gain,
    cached_pool,
    route,
    queries,
    shortlist,
    teacher,
):
    section = lax.axis_index("section")
    sections = lax.axis_size("section")
    dp = lax.axis_index("dp")
    dps = lax.axis_size("dp")
    half = dps // 2
    side, place = dp % 2, dp // 2
    weight = section_weight[0]
    gain = section_gain[0]
    width, cols = weight.shape
    tok = held_states.shape[1]
    pair_rows = 2 * tok

    def send(x, hops):
        return lax.ppermute(
            x, AXES, [(a * dps + i, b * dps + (i ^ flip)) for a, b, flip in hops for i in range(dps)]
        )

    def rows_at(x, index):
        return x.at[index].get(mode="promise_in_bounds")

    flips = jnp.where(section == 0, 0, place)
    last_full = sections - 1 - TICKS

    def split_weights(order, firsts):
        theirs = gained_blocks(weight, gain, 2 * order + 1 - side)
        mine = gained_blocks(weight, gain, 2 * order + side)
        rest = [a for a in range(sections - 1) if a not in firsts]
        came = send(theirs, [(a, a, 1) for a in firsts])
        if rest:
            later = send(theirs, [(a, a, 1) for a in rest])
        else:
            later = came
        return mine, came, jnp.where(section <= max(firsts), came, later)

    mine_late, theirs_first, theirs_late = split_weights(
        jnp.arange(half) ^ flips, list(range(last_full + 1))
    )
    mine_first = mine_late
    if last_full > 0:
        mine_first, _, theirs_first = split_weights(
            jnp.arange(half), list(range(last_full + 1))
        )

    helper = sections - TICKS + 1
    used = list(range(last_full + 1)) + [helper]

    def sides(x):
        pieces = [x[:, k * cols : (k + 1) * cols] for k in range(dps)]
        even, odd = jnp.concatenate(pieces[0::2], axis=1), jnp.concatenate(pieces[1::2], axis=1)
        return jnp.where(side == 0, even, odd), jnp.where(side == 0, odd, even)

    def fan(x, pairs, steps):
        got = {}
        for k in sorted(steps, key=lambda k: (k != half // 2, k == 0, k)):
            got[k] = send(x, [(a, b, 2 * k) for a, b in pairs])
        return [got[k] for k in steps]

    def gathered(x, owners):
        here, leave = sides(x)
        there = send(leave, [(a, a, 1) for a in owners])
        pair = jnp.where(
            side == 0,
            jnp.concatenate([here, there], axis=0),
            jnp.concatenate([there, here], axis=0),
        )
        return [pair] + fan(pair, [(a, a) for a in owners], range(1, half))

    entry = jnp.where(section == helper, fresh_batches[0], held_states[0])
    entry_piles = gathered(entry, used)
    fresh_piles = [gathered(fresh_batches[i], [0]) for i in range(1, TICKS - 1)]

    rows = cached_pool.shape[0]
    per_peer = rows // dps
    last_token = held_states[0, tok - 1].reshape(1, per_peer, width // per_peer)
    outbox = jnp.concatenate(
        [
            rows_at(cached_pool, route[0]).reshape(dps, per_peer, width),
            jnp.broadcast_to(last_token, (dps, per_peer, width // per_peer)),
            jnp.broadcast_to(
                route[0].astype(jnp.bfloat16).reshape(dps, per_peer, 1), (dps, per_peer, 128)
            ),
        ],
        axis=2,
    )
    inbox = lax.all_to_all(outbox, "dp", split_axis=0, concat_axis=0)
    owner_queries = lax.all_gather(queries, "section", axis=0, tiled=True)

    def layer(row_piles, column_piles, mine, theirs, at, hops):
        at = jnp.stack([jnp.asarray(x, jnp.int32) for x in at])
        part, square, states = sent_half(at, row_piles, column_piles, theirs)
        other = send(part, hops)
        return kept_half(at, states, mine, other, square, width, pair_rows), states

    block, states = layer(
        entry_piles,
        [],
        mine_first,
        theirs_first,
        (1, place, place),
        [(a, a, 1) for a in range(last_full + 1)],
    )
    fresh_piles.insert(0, [send(states, [(helper, 0, 0)])])
    first = section == 0
    row_order = jnp.where(first, place, 0)
    for tick in range(1, TICKS):
        top = last_full + tick
        if tick == 1:
            piles = fan(block, [(a - 1, a) for a in range(1, top + 1)], range(half))
        else:
            block = send(block, [(a - 1, a, 0) for a in range(1, top + 1)])
            piles = [block] + fan(block, [(a, a) for a in range(1, top + 1)], range(1, half))
        block, _ = layer(
            fresh_piles[tick - 1],
            piles,
            mine_late,
            theirs_late,
            (first, row_order, row_order),
            [(a, a, 1) for a in range(top + 1)],
        )
    tokens = lax.all_to_all(block, "dp", split_axis=0, concat_axis=1, tiled=True)
    shifted = send(tokens, [(a, a + 1, 0) for a in range(sections - 1)])
    held_out = jnp.where(section == 0, fresh_batches[TICKS - 1], shifted)[None]

    def spread(x):
        pieces = lax.all_to_all(
            jnp.broadcast_to(x[None], (dps, *x.shape)), "dp", split_axis=0, concat_axis=0
        )
        return jnp.transpose(pieces, (1, 0, 2)).reshape(x.shape[0], width)

    every = SEQ // tok
    ends = inbox[every - 1 :: every, :, width : width + width // per_peer].reshape(-1, width)
    exits = []
    for tick in range(TICKS):
        wide = ends.astype(jnp.float32)
        inv_rms = lax.rsqrt(jnp.mean(wide * wide, axis=-1, keepdims=True) + epsilon)
        normed = (wide * inv_rms * gain).astype(jnp.bfloat16)
        projected = jnp.dot(normed, weight, preferred_element_type=jnp.float32)
        projected = projected.astype(jnp.bfloat16).astype(jnp.float32)
        kept = lax.dynamic_slice_in_dim(wide, dp * cols, cols, axis=1)
        piece = (kept + jax.nn.silu(projected)).astype(jnp.bfloat16)
        exits.append(piece)
        if tick < TICKS - 1:
            piece = send(
                piece, [(a, a + 1, 0) for a in range(sections - TICKS + tick, sections - 1)]
            )
            ends = spread(piece)
    passages = ends.shape[0]
    exit_pieces = lax.all_gather(jnp.concatenate(exits, axis=0), "section", axis=0)
    exit_rows = spread(exit_pieces[sections - 1])
    scaled = exit_rows.astype(jnp.float32) * final_gain
    embedded = (
        scaled * lax.rsqrt(jnp.sum(scaled * scaled, axis=-1, keepdims=True) + epsilon)
    ).astype(jnp.bfloat16)

    source = jnp.arange(rows) // per_peer
    passage = source // every
    is_end = source % every == every - 1
    slot = inbox[:, :, width + width // per_peer].reshape(rows).astype(jnp.int32)
    replaced = is_end & (slot < TICKS)
    pick = jnp.where(replaced, slot * passages + passage, -1)
    chosen = (pick[:, None] == jnp.arange(TICKS * passages)).astype(jnp.bfloat16)
    received = jnp.where(
        replaced[:, None],
        jnp.dot(chosen, embedded, preferred_element_type=jnp.float32).astype(jnp.bfloat16),
        inbox[:, :, :width].reshape(rows, width),
    )
    all_scores = lax.dot_general(
        queries, received, (((1,), (1,)), ((), ())), preferred_element_type=jnp.float32
    )
    listed = shortlist[..., None] == jnp.arange(rows, dtype=jnp.int32)
    student = jnp.sum(jnp.where(listed, all_scores[:, None, :], 0.0), axis=-1) * logit_scale
    student_log = jax.nn.log_softmax(student, axis=-1)
    teacher_log = jax.nn.log_softmax(teacher, axis=-1)
    teacher_prob = jnp.exp(teacher_log)
    losses = jnp.sum(teacher_prob * (teacher_log - student_log), axis=-1)
    logit_grad = logit_scale * (jnp.exp(student_log) - teacher_prob)
    row_grad = jnp.sum(jnp.where(listed, logit_grad[..., None], 0.0), axis=1)
    received_wide = received.astype(jnp.float32)
    owner_grads = lax.all_gather(row_grad, "section", axis=0, tiled=True)
    received_grad = jnp.dot(
        owner_grads.T, owner_queries.astype(jnp.float32), precision=lax.Precision.HIGHEST
    ).astype(jnp.bfloat16)
    query_grad = jnp.dot(row_grad, received_wide, precision=lax.Precision.HIGHEST)
    returned = lax.all_to_all(received_grad, "dp", split_axis=0, concat_axis=0, tiled=True)
    spots = jnp.arange(rows)
    back = jnp.sum(jnp.where(route[0][None, :] == spots[:, None], spots[None, :], 0), axis=1)
    pool_grad = rows_at(returned, back)
    return (held_out, losses, query_grad, pool_grad)


def solution(mesh):
    return jax.shard_map(
        on_device,
        mesh=mesh,
        in_specs=(
            P(None, "dp", None),
            P("section", "dp", None),
            P("section", None, "dp"),
            P("section", None),
            P(),
            P("dp", None),
            P("dp", None),
            P(("section", "dp"), None),
            P(("section", "dp"), None),
            P(("section", "dp"), None),
        ),
        out_specs=(
            P("section", "dp", None),
            P(("section", "dp")),
            P(("section", "dp"), None),
            P("dp", None),
        ),
        check_vma=False,
    )
```
